128 devices in a mesh: slab: 16 (over y, z), brick: 8 (over x, core).
Axes of the slice: x: 4, y: 4, z: 4, core: 2. Of those that a mesh axis runs over, the one named last changes fastest.
Arguments:
- positions: float32 [8192, 3, 128], P(('slab', 'brick')), may hold values from -6 to 6
- velocities: float32 [8192, 3, 128], P(('slab', 'brick')), may hold values from -6 to 6
- radii: float32 [8192, 128], P(('slab', 'brick')), may hold values from 0.6 to 1.2
- cell_of: int32 [8192, 128], P(('slab', 'brick')), may hold values from 0 to 65535
- block_route: int32 [8192, 1], P(('slab', 'brick')), may hold values from 0 to 23; in each aligned block of 64 rows (0 to 63, 64 to 127, ...) at most 6 rows name the same one
- ghost_list: int32 [2048], P(('slab', 'brick')), may hold values from 0 to 63
- tile_home: int32 [16384], P(('slab', 'brick')), may hold values from 0 to 63
- tile_partner: int32 [16384], P(('slab', 'brick')), may hold values from 0 to 95
- fluid: float32 [3, 64, 256, 512], P(None, 'slab', 'brick'), may hold values from -6 to 6
Outputs:
- velocity_next: float32 [8192, 3, 128], P(('slab', 'brick'))
- fluid_next: float32 [3, 64, 256, 512], P(None, 'slab', 'brick')
The draws below stay inside these ranges and needn't reach their ends.
Inputs may be any that keep to these rules, and one draw needn't show every extreme that they name: `block_route`: within the blocks of one device no code appears more than 6 times, and some device's blocks reach 6 for some code.
All inputs are finite; a program needn't handle non-finite values.
Results may differ from the reference program's by a relative error of at most 0.00013.
Values sent between devices are 32-bit elements; how exact they have to be, the bound alone decides.
A program may use at most 64 MiB of HBM per device.

```python
import math
import jax
import jax.numpy as jnp
import numpy as np
from jax import lax

BLK = 128
NB = 64
GH = 4
CX = 4
CY = 32
CZ = 512
TILES = 128
CAP = 6
BLOCKS = 8192
CELLS = 65536
NX = 64
NY = 256
N_SLAB = 16
N_BRICK = 8


def set_ends(values, rng, smallest, top_value):
    spot = [jax.random.randint(jax.random.fold_in(rng, axis), (), 0, length) for axis, length in enumerate(values.shape)]
    longest = values.shape.index(max(values.shape))
    next_to = spot[:longest] + [(spot[longest] + 1) % values.shape[longest]] + spot[longest + 1:]
    return values.at[tuple(spot)].set(smallest).at[tuple(next_to)].set(top_value)


def levels(own_key, extent, shards, smallest, top_value):
    def one(position, shards_of):
        steps = jax.random.uniform(jax.random.fold_in(jax.random.fold_in(own_key, 6), position), (shards_of,), jnp.float32, smallest / len(shards), top_value / len(shards))
        return jnp.repeat(jnp.exp(steps), extent[position] // shards_of).reshape((-1,) + (1,) * (len(extent) - position - 1))

    factor_of = one(*shards[0])
    for cut in shards[1:]:
        factor_of = factor_of * one(*cut)
    return factor_of


def assign_block(own_key, own, number, rows, amount, top, bound, skew):
    order = jax.random.permutation(own_key, amount)
    crowded, ordinary = load_shares(amount, rows * top, bound, skew, True), load_shares(amount, rows * top, bound, skew, False)
    places = jnp.arange(amount)

    def named(lengths, rotation):
        used = int((lengths > 0).sum())
        fixed = max(1, used // 4)
        moved = fixed + (places - fixed + rotation * (used - fixed)) % max(1, amount - fixed)
        return jnp.zeros((amount,), jnp.int32).at[order[jnp.where(places < fixed, places, moved)]].set(jnp.asarray(lengths, jnp.int32))

    lengths = jnp.where(number % 4 == 0, named(crowded, number // 4), named(ordinary, number - number // 4 - 1))
    mixed = jax.random.permutation(jax.random.fold_in(own, 3), amount)
    donor, sink = mixed[0:amount // 2 * 2:2], mixed[1:amount // 2 * 2:2]
    room = jnp.minimum(lengths[donor] - 1, bound - lengths[sink]) // 2
    room = jnp.where((donor == order[0]) | (sink == order[0]) | (lengths[sink] == 0), 0, jnp.maximum(room, 0))
    moved = jax.random.randint(jax.random.fold_in(own, 4), (amount // 2,), 0, 1 << 20) % (room + 1)
    lengths = lengths.at[donor].add(-moved).at[sink].add(moved)
    members = jnp.searchsorted(jnp.cumsum(lengths), jnp.arange(rows * top), side="right").astype(jnp.int32)
    grid = members.reshape(top, rows).T
    grid = grid[jax.random.permutation(jax.random.fold_in(own, 1), rows)]
    rotation = jax.random.randint(jax.random.fold_in(own, 2), (rows, 1), 0, top)
    return jnp.take_along_axis(grid, (jnp.arange(top)[None, :] + rotation) % top, axis=1)


def load_shares(amount, total, limit, lean, full):
    weights = [(1 << 20) // math.isqrt(grade ** lean) + 1 for grade in range(1, amount + 1)]
    largest = limit if full else min(limit, max(-(-total // amount), total * weights[0] // sum(weights)))
    least = 1 if total - largest >= amount - 1 else 0
    given, spare = [largest] + [least] * (amount - 1), total - largest - least * (amount - 1)
    while spare > 0:
        movable = [i for i in range(1, amount) if given[i] < largest] or [i for i in range(1, amount) if given[i] < limit]
        pool, remaining = sum([weights[i] for i in movable]), spare
        for i in movable:
            extra = min(limit - given[i], max(1, remaining * weights[i] // pool), spare)
            given[i] = given[i] + extra
            spare = spare - extra
    return np.array(given)


def normal_values(own_key, extent, deviation, limit, shards=(), kind=jnp.bfloat16):
    values = jax.random.normal(own_key, extent, jnp.float32) * deviation
    if len(shards) > 0:
        values = levels(own_key, extent, shards, -0.22, 0.18) * values
    return jnp.clip(values, min=-limit, max=limit).astype(kind)


def setup_inputs(seed: int = 0) -> dict:
    key_of = jax.random.split(jax.random.key(seed), 10)
    positions = normal_values(key_of[0], (BLOCKS, 3, BLK), 1.0, 6.0, ((0, 128),), jnp.float32)
    velocities = normal_values(key_of[1], (BLOCKS, 3, BLK), 1.0, 6.0, ((0, 128),), jnp.float32)
    radii = jnp.clip(0.6 + 0.6 * jax.random.uniform(key_of[2], (BLOCKS, BLK), jnp.float32) ** levels(key_of[2], (BLOCKS, BLK), ((0, 128),), -0.2, 0.2), 0.6, 1.2)
    cell_of = set_ends(jax.random.randint(key_of[3], (BLOCKS, BLK), 0, CELLS), jax.random.fold_in(key_of[3], 1), 0, CELLS - 1).astype(jnp.int32)
    block_route_keys = jax.random.split(jax.random.fold_in(key_of[4], 1), BLOCKS // NB)
    block_route_turns = jax.random.permutation(jax.random.fold_in(key_of[4], 3), BLOCKS // NB)
    block_route = jax.vmap(lambda own, number: assign_block(jax.random.fold_in(key_of[4], 2), own, number, NB, 3 * N_BRICK, 1, CAP, 2))(block_route_keys, block_route_turns).reshape((BLOCKS, 1))
    ghost_list = set_ends(jax.random.randint(key_of[5], (N_SLAB * N_BRICK * 4 * GH,), 0, NB), jax.random.fold_in(key_of[5], 1), 0, NB - 1).astype(jnp.int32)
    tile_home = set_ends(jax.random.randint(key_of[6], (N_SLAB * N_BRICK * TILES,), 0, NB), jax.random.fold_in(key_of[6], 1), 0, NB - 1).astype(jnp.int32)
    tile_partner = set_ends(jax.random.randint(key_of[7], (N_SLAB * N_BRICK * TILES,), 0, NB + 8 * GH), jax.random.fold_in(key_of[7], 1), 0, (NB + 8 * GH) - 1).astype(jnp.int32)
    fluid = normal_values(key_of[8], (3, NX, NY, CZ), 1.0, 6.0, ((1, 16), (2, 8)), jnp.float32)
    return {"positions": positions, "velocities": velocities, "radii": radii, "cell_of": cell_of, "block_route": block_route, "ghost_list": ghost_list, "tile_home": tile_home, "tile_partner": tile_partner, "fluid": fluid}


stiffness = 0.01
damping = 0.005
viscosity = 0.1
coupling = 0.5
relaxation = 0.5


def pack_blocks(positions, velocities, radii):
    return jnp.concatenate([positions, velocities, radii[:, None, :]], axis=1)


def tile_forces(home_block, partner):
    here_pos = home_block[:, 0:3]
    there_pos = partner[:, 0:3]
    here_vel = home_block[:, 3:6]
    there_vel = partner[:, 3:6]
    offsets = here_pos[:, :, :, None] - there_pos[:, :, None, :]
    squared = jnp.sum(offsets * offsets, axis=1)
    contact = home_block[:, 6, :, None] + partner[:, 6, None, :]
    weight = jnp.maximum(contact * contact - squared, 0.0)
    weight_sum = jnp.sum(weight, axis=2)
    spring = jnp.sum(weight[:, None] * offsets, axis=3)
    friction = jnp.einsum("bij,bcj->bci", weight, there_vel, precision=lax.Precision.HIGHEST) - here_vel * weight_sum[:, None]
    return stiffness * spring + damping * friction


def contact_forces(candidates, homes, partners, nblocks):
    width = candidates.shape[2]
    group = math.gcd(homes.shape[0], 16)
    home_groups = homes.reshape(-1, group)
    partner_groups = partners.reshape(-1, group)

    def advance_tiles(accumulated, indices):
        home_ids, partner_ids = indices
        terms = tile_forces(candidates[home_ids], candidates[partner_ids])
        return accumulated.at[home_ids].add(terms), None

    start = jnp.zeros((nblocks, 3, width), jnp.float32)
    result, _ = lax.scan(advance_tiles, start, (home_groups, partner_groups))
    return result


def laplacian_grid(field):
    padded_z = jnp.pad(field, ((0, 0), (0, 0), (0, 0), (1, 1)))
    inner = padded_z[:, :, :, 1:-1]
    total = jnp.roll(field, -1, axis=1) + jnp.roll(field, 1, axis=1)
    total = total + jnp.roll(field, -1, axis=2) + jnp.roll(field, 1, axis=2)
    total = total + padded_z[:, :, :, 2:] + padded_z[:, :, :, :-2]
    return total - 6.0 * inner


def reference(positions, velocities, radii, cell_of, block_route, ghost_list, tile_home, tile_partner, fluid):
    ndev = N_SLAB * N_BRICK
    packed = pack_blocks(positions, velocities, radii).reshape(ndev, NB, 7, BLK)
    ghost_ids = ghost_list.reshape(ndev, 4 * GH)
    ghost_sets = jax.vmap(lambda blocks, ids: blocks[ids])(packed, ghost_ids).reshape(ndev, 2, 2, GH, 7, BLK)
    devices_all = jnp.arange(ndev, dtype=jnp.int32)
    slab_of = devices_all // N_BRICK
    brick_of = devices_all % N_BRICK
    lower_slab = ((slab_of - 1) % N_SLAB) * N_BRICK + brick_of
    upper_slab = ((slab_of + 1) % N_SLAB) * N_BRICK + brick_of
    lower_brick = slab_of * N_BRICK + (brick_of - 1) % N_BRICK
    upper_brick = slab_of * N_BRICK + (brick_of + 1) % N_BRICK
    homes_all = tile_home.reshape(ndev, TILES)
    partners_all = tile_partner.reshape(ndev, TILES)

    def one_device(device):
        candidates = jnp.concatenate([
            packed[device],
            ghost_sets[lower_slab[device]][1].reshape(-1, 7, BLK),
            ghost_sets[upper_slab[device]][0].reshape(-1, 7, BLK),
            ghost_sets[lower_brick[device]][:, 1].reshape(-1, 7, BLK),
            ghost_sets[upper_brick[device]][:, 0].reshape(-1, 7, BLK)], axis=0)
        return contact_forces(candidates, homes_all[device], partners_all[device], NB)

    forces = lax.map(one_device, devices_all).reshape(BLOCKS, 3, BLK)
    masses = radii * radii * radii
    updated = velocities + forces / masses[:, None, :]
    route_code = block_route[:, 0]
    block_slab = jnp.repeat(slab_of, NB)
    destination = ((block_slab + route_code // N_BRICK - 1) % N_SLAB) * N_BRICK + route_code % N_BRICK
    cell_global = (destination[:, None] * CELLS + cell_of).reshape(-1)
    volume = jnp.zeros((ndev * CELLS,), jnp.float32).at[cell_global].add(masses.reshape(-1))
    carried = jnp.moveaxis(masses[:, None, :] * updated, 1, 0).reshape(3, -1)
    momentum = jnp.zeros((3, ndev * CELLS), jnp.float32).at[:, cell_global].add(carried)

    def to_grid(flat):
        chans = flat.shape[0]
        shaped = flat.reshape(chans, N_SLAB, N_BRICK, CX, CY, CZ).transpose(0, 1, 3, 2, 4, 5)
        return shaped.reshape(chans, NX, NY, CZ)

    volume_grid = to_grid(volume[None])
    momentum_grid = to_grid(momentum)
    fluid_next = fluid + viscosity * laplacian_grid(fluid) + coupling * (momentum_grid - volume_grid * fluid)
    back_flat = fluid_next.reshape(3, N_SLAB, CX, N_BRICK, CY, CZ).transpose(0, 1, 3, 2, 4, 5).reshape(3, -1)
    sampled = jnp.moveaxis(back_flat[:, cell_global].reshape(3, BLOCKS, BLK), 0, 1)
    velocity_next = updated + relaxation * (sampled - updated)
    return velocity_next, fluid_next
```

```python
import functools

import jax
import jax.numpy as jnp
from jax import lax
from jax.experimental import pallas as pl
from jax.experimental.pallas import tpu as pltpu
from jax.sharding import PartitionSpec as P

stiffness = 0.01
damping = 0.005
viscosity = 0.1
coupling = 0.5
relaxation = 0.5

MESH = pl.DeviceIdType.MESH
F32 = jnp.float32
BF16 = jnp.bfloat16
VMEM = pl.BlockSpec(memory_space=pltpu.VMEM)
SMEM = pl.BlockSpec(memory_space=pltpu.SMEM)

N_SLAB = 16
N_BRICK = 8
NB = 64
BLK = 128
TILES = 128
CAND = 96
CODES = 24
CAP = 6
SEND_ROWS = 32
BACK_ROWS = 24
COLS = 128
DEPTH = 512
CHUNK = 2


def iota(shape, dim, dtype=jnp.int32):
    return lax.broadcasted_iota(jnp.int32, shape, dim).astype(dtype)


def split3(x):
    high = x.astype(BF16)
    rest = x - high.astype(F32)
    middle = rest.astype(BF16)
    low = (rest - middle.astype(F32)).astype(BF16)
    return high, middle, low


def split2(x):
    high = x.astype(BF16)
    return high, (x - high.astype(F32)).astype(BF16)


def params(mib, collective_id=None):
    return pltpu.CompilerParams(
        vmem_limit_bytes=mib << 20,
        collective_id=collective_id,
        has_side_effects=collective_id is not None,
    )


def halo_kernel(
    glist, pos, vel, rad, fluid, ghosts, xlo, xhi, ylo, yhi, gsend, ysend, send_sem, recv_sem
):
    s, b = lax.axis_index("slab"), lax.axis_index("brick")
    upper_s = (lax.rem(s + 1, N_SLAB), b)
    lower_s = (lax.rem(s + N_SLAB - 1, N_SLAB), b)
    upper_b = (s, lax.rem(b + 1, N_BRICK))
    lower_b = (s, lax.rem(b + N_BRICK - 1, N_BRICK))
    barrier = pltpu.get_barrier_semaphore()
    for peer in (upper_s, lower_s, upper_b, lower_b):
        pl.semaphore_signal(barrier, inc=1, device_id=peer, device_id_type=MESH)
    for g in range(16):
        source = glist[g]
        i, j, k = g // 8, g // 4 % 2, g % 4
        for c in range(3):
            gsend[i, j, k, c : c + 1, :] = pos[c, pl.ds(source, 1), :]
            gsend[i, j, k, 3 + c : 4 + c, :] = vel[c, pl.ds(source, 1), :]
        gsend[i, j, k, 6:7, :] = rad[pl.ds(source, 1), :]
        gsend[i, j, k, 7:8, :] = jnp.zeros((1, BLK), F32)
    for c in range(3):
        for ix in range(4):
            row = c * 4 + ix
            ysend[0, row : row + 1, :] = fluid[c, ix, 0:1, :]
            ysend[1, row : row + 1, :] = fluid[c, ix, 31:32, :]
    pl.semaphore_wait(barrier, 4)
    plan = (
        (gsend.at[1], ghosts.at[0], upper_s),
        (gsend.at[0], ghosts.at[1], lower_s),
        (gsend.at[:, 1], ghosts.at[2], upper_b),
        (gsend.at[:, 0], ghosts.at[3], lower_b),
        (fluid.at[:, 3], xlo, upper_s),
        (fluid.at[:, 0], xhi, lower_s),
        (ysend.at[1], ylo, upper_b),
        (ysend.at[0], yhi, lower_b),
    )
    copies = [
        pltpu.make_async_remote_copy(
            src_ref=src,
            dst_ref=dst,
            send_sem=send_sem.at[n],
            recv_sem=recv_sem.at[n],
            device_id=peer,
            device_id_type=MESH,
        )
        for n, (src, dst, peer) in enumerate(plan)
    ]
    for copy in copies:
        copy.start()
    for copy in copies:
        copy.wait()


def halo_exchange(glist, pos, vel, rad, fluid):
    sds = jax.ShapeDtypeStruct
    return pl.pallas_call(
        halo_kernel,
        out_shape=(
            sds((4, 2, 4, 8, BLK), F32),
            sds((3, 32, DEPTH), F32),
            sds((3, 32, DEPTH), F32),
            sds((16, DEPTH), F32),
            sds((16, DEPTH), F32),
        ),
        in_specs=[SMEM, VMEM, VMEM, VMEM, VMEM],
        out_specs=(VMEM,) * 5,
        scratch_shapes=[
            pltpu.VMEM((2, 2, 4, 8, BLK), F32),
            pltpu.VMEM((2, 16, DEPTH), F32),
            pltpu.SemaphoreType.DMA((8,)),
            pltpu.SemaphoreType.DMA((8,)),
        ],
        compiler_params=params(32, 0),
    )(glist, pos, vel, rad, fluid)


def contact_kernel(
    home,
    partner,
    pos,
    vel,
    rad,
    cell,
    route,
    ghosts,
    updated,
    slots,
    outgoing,
    cand,
    jfeat,
    ifeat,
    afeat,
    total,
    payload,
):
    for c in range(3):
        cand[0:NB, c, :] = pos[c]
        cand[0:NB, 3 + c, :] = vel[c]
    cand[0:NB, 6, :] = rad[...]
    cand[0:NB, 7, :] = jnp.zeros((NB, BLK), F32)
    cand[NB:CAND] = ghosts[...]
    total[...] = jnp.zeros_like(total)
    row = iota((8, BLK), 0)

    def features(n, _):
        q = cand[n]
        radius = q[6:7]
        q4 = jnp.where(row < 3, q, jnp.where(row == 3, radius, 0.0))
        square = q4 * q4
        p = jnp.sum(jnp.where(row == 3, square, -square), axis=0, keepdims=True)
        jt = jnp.where(row == 4, p, jnp.where(row == 5, 1.0, q4))
        it = jnp.where(row == 5, p, jnp.where(row == 4, 1.0, 2.0 * q4))
        speed = pltpu.roll(q, 5, 0)
        at = jnp.where(
            row < 3, stiffness * q - damping * speed, jnp.where(row == 3, 1.0, 0.0)
        )
        jh, jm, jl = (x.astype(F32) for x in split3(jt))
        ih, im, il = (x.astype(F32) for x in split3(it))
        ah, am, al = (x.astype(F32) for x in split3(at))
        jfeat[n] = jnp.concatenate([jh, jh, jm, jh, jl, jm], axis=0).astype(BF16)
        ifeat[n] = jnp.concatenate([ih, im, ih, il, ih, im], axis=0).astype(BF16)
        a = jnp.concatenate([ah, am, al, jnp.zeros_like(al)], axis=0).astype(BF16)
        afeat[n] = jnp.concatenate([a, a], axis=1)
        return 0

    lax.fori_loop(0, CAND, features, 0, unroll=8)

    def tile_sum(t):
        h, p = home[t], partner[t]
        s = lax.dot_general(
            jfeat[p], ifeat[h], (((0,), (0,)), ((), ())), preferred_element_type=F32
        )
        high, low = split2(jnp.maximum(s, 0.0))
        weight = jnp.concatenate([high, low], axis=0)
        out = jnp.dot(afeat[p], weight, preferred_element_type=F32)
        return h, out[0:8] + out[8:16] + out[16:24]

    def tiles(step, _):
        results = [tile_sum(step * 8 + n) for n in range(8)]
        for h, value in results:
            total[h] += value
        return 0

    lax.fori_loop(0, TILES // 8, tiles, 0)

    r = rad[...]
    mass = r * r * r
    weight_sum = total[:, 3, :]
    parts = [r]
    for c in range(3):
        a = stiffness * pos[c] - damping * vel[c]
        force = a * weight_sum - total[:, c, :]
        value = vel[c] + force / mass
        updated[c] = value
        parts.append(value)
    parts.append(cell[...].astype(F32) + 1.0)
    parts.append(jnp.zeros((NB, BLK), F32))
    for c, part in enumerate(parts):
        high, middle, low = split3(part)
        payload[c * NB : (c + 1) * NB, 0:BLK] = high
        payload[c * NB : (c + 1) * NB, BLK : 2 * BLK] = middle
        payload[c * NB : (c + 1) * NB, 2 * BLK : 3 * BLK] = low

    code = jnp.concatenate([route[...], route[...]], axis=1).astype(F32)
    lanes = jnp.broadcast_to(code, (BLK, BLK))
    across = jnp.transpose(lanes)
    sub, lane = iota((BLK, BLK), 0), iota((BLK, BLK), 1)
    earlier = (across == lanes) & (sub < NB) & (sub < lane % NB)
    before = jnp.sum(jnp.where(earlier, 1.0, 0.0), axis=0, keepdims=True)
    slot = code * CAP + before
    slots[...] = jnp.broadcast_to(slot, (8, BLK)).astype(jnp.int32)
    slot_i = slot.astype(jnp.int32)
    lane_row = iota((1, BLK), 1)
    upper_half = jnp.where(lane_row >= NB, 1, 0)
    key = jnp.concatenate([slot_i * 8 + 2 * g + upper_half for g in range(3)], axis=1)

    per = 192
    for part in range(CODES * SEND_ROWS // per):
        rho = iota((per, 3 * BLK), 0) + part * per
        q = rho % SEND_ROWS
        want = ((rho // SEND_ROWS) * CAP + q // 5) * 8 + q % 5
        want = jnp.where(q < 5 * CAP, want, -1)
        hot = jnp.where(want == key, 1.0, 0.0).astype(BF16)
        out = jnp.dot(hot, payload[...], preferred_element_type=F32)
        outgoing[part * per : (part + 1) * per, :] = (
            out[:, 0:BLK] + out[:, BLK : 2 * BLK] + out[:, 2 * BLK : 3 * BLK]
        )


def contacts(home, partner, pos, vel, rad, cell, route, ghosts):
    sds = jax.ShapeDtypeStruct
    return pl.pallas_call(
        contact_kernel,
        out_shape=(
            sds((3, NB, BLK), F32),
            sds((8, BLK), jnp.int32),
            sds((CODES * SEND_ROWS, BLK), F32),
        ),
        in_specs=[SMEM, SMEM] + [VMEM] * 6,
        out_specs=(VMEM,) * 3,
        scratch_shapes=[
            pltpu.VMEM((CAND, 8, BLK), F32),
            pltpu.VMEM((CAND, 48, BLK), BF16),
            pltpu.VMEM((CAND, 48, BLK), BF16),
            pltpu.VMEM((CAND, 32, 2 * BLK), BF16),
            pltpu.VMEM((NB, 8, BLK), F32),
            pltpu.VMEM((6 * NB, 3 * BLK), BF16),
        ],
        compiler_params=params(48),
    )(home, partner, pos, vel, rad, cell, route, ghosts)


def send_all(src, dst, send_sem, recv_sem, local_sem, rows, sign):
    s, b = lax.axis_index("slab"), lax.axis_index("brick")

    def region(index):
        return pl.ds(pl.multiple_of(index * rows, 8), rows)

    copies = []
    for turn in range(N_BRICK):
        brick = lax.rem(b + turn, N_BRICK)
        for o in range(3):
            slab = lax.rem(s + N_SLAB + sign * (o - 1), N_SLAB)
            n = turn * 3 + o
            source = src.at[region(o * N_BRICK + brick)]
            target = dst.at[region(o * N_BRICK + b)]
            if turn == 0 and o == 1:
                copies.append(pltpu.make_async_copy(source, target, local_sem))
            else:
                copies.append(
                    pltpu.make_async_remote_copy(
                        src_ref=source,
                        dst_ref=target,
                        send_sem=send_sem.at[n],
                        recv_sem=recv_sem.at[n],
                        device_id=(slab, brick),
                        device_id_type=MESH,
                    )
                )
    return copies


def greet_all(barrier):
    s, b = lax.axis_index("slab"), lax.axis_index("brick")
    for turn in range(N_BRICK):
        for o in range(3):
            if turn == 0 and o == 1:
                continue
            peer = (lax.rem(s + N_SLAB + o - 1, N_SLAB), lax.rem(b + turn, N_BRICK))
            pl.semaphore_signal(barrier, inc=1, device_id=peer, device_id_type=MESH)
    pl.semaphore_wait(barrier, 3 * N_BRICK - 1)


def route_kernel(src, dst, send_sem, recv_sem, local_sem):
    greet_all(pltpu.get_barrier_semaphore())
    copies = send_all(src, dst, send_sem, recv_sem, local_sem, SEND_ROWS, 1)
    for copy in copies:
        copy.start()
    for copy in copies:
        copy.wait()


def route_blocks(outgoing):
    return pl.pallas_call(
        route_kernel,
        out_shape=jax.ShapeDtypeStruct(outgoing.shape, F32),
        in_specs=[VMEM],
        out_specs=VMEM,
        scratch_shapes=[
            pltpu.SemaphoreType.DMA((CODES,)),
            pltpu.SemaphoreType.DMA((CODES,)),
            pltpu.SemaphoreType.DMA,
        ],
        compiler_params=params(32, 1),
    )(outgoing)


def return_kernel(slots, updated, src, out, back, send_sem, recv_sem, local_sem):
    greet_all(pltpu.get_barrier_semaphore())
    copies = send_all(src, back, send_sem, recv_sem, local_sem, BACK_ROWS, -1)
    for copy in copies:
        copy.start()
    for copy in copies:
        copy.wait()
    for n in range(NB):
        slot = slots[0, n]
        first = (slot // CAP) * BACK_ROWS + (slot % CAP) * 3
        for c in range(3):
            here = updated[c, n : n + 1, :]
            picked = back[pl.ds(first + c, 1), :]
            out[c, n : n + 1, :] = here + relaxation * (picked - here)


def return_answers(slots, updated, answers):
    return pl.pallas_call(
        return_kernel,
        out_shape=jax.ShapeDtypeStruct((3, NB, BLK), F32),
        in_specs=[SMEM, VMEM, VMEM],
        out_specs=VMEM,
        scratch_shapes=[
            pltpu.VMEM((CODES * BACK_ROWS, BLK), F32),
            pltpu.SemaphoreType.DMA((CODES,)),
            pltpu.SemaphoreType.DMA((CODES,)),
            pltpu.SemaphoreType.DMA,
        ],
        compiler_params=params(32, 2),
    )(slots, updated, answers)


def fluid_kernel(
    arrived, fluid, xlo, xhi, ylo, yhi, fluid_next, answers, blocks, sampled, acc, halves
):
    offset = []
    at = jnp.int32(0)
    valid = jnp.zeros((CODES, 1), F32)
    for k in range(CAP):
        cells = arrived[pl.ds(5 * k + 4, CODES, stride=SEND_ROWS), :]
        valid = valid + jnp.where(cells[:, 0:1] > 0.5, 1.0, 0.0)
    counted = valid.astype(jnp.int32)
    for d in range(CODES):
        offset.append(at)
        at = at + counted[d, 0]
    total = at
    blank = jnp.zeros((8, BLK), F32)
    for d in range(CODES):
        for k in range(CAP):
            base = d * SEND_ROWS + 5 * k
            blocks[offset[d] + k, 0:5, :] = arrived[base : base + 5, :]
    for n in range(CHUNK):
        blocks[total + n] = blank
    steps = (total + CHUNK - 1) // CHUNK
    acc[...] = jnp.zeros_like(acc)

    col_iota = iota((COLS, BLK), 0)
    z_sub = iota((DEPTH, BLK), 0)
    z_lane = iota((BLK, DEPTH), 1)

    def deposit(step, _):
        left, right = [], []
        for n in range(CHUNK):
            tile = blocks[step * CHUNK + n]
            cell = tile[4:5].astype(jnp.int32) - 1
            col, level = cell >> 9, cell & (DEPTH - 1)
            radius = tile[0:1]
            mass = radius * radius * radius
            hot = jnp.where(col_iota == col, 1.0, 0.0).astype(BF16)
            loads = [mass] + [mass * tile[1 + c : 2 + c] for c in range(3)]
            pieces = [split2(x) for x in loads]
            for which in range(2):
                left.append(jnp.concatenate([hot * p[which] for p in pieces], axis=0))
            depth_tile = jnp.broadcast_to(level.astype(F32), (BLK, BLK))
            column = jnp.transpose(depth_tile).astype(jnp.int32)
            wide = jnp.concatenate([column] * (DEPTH // BLK), axis=1)
            z_hot = jnp.where(wide == z_lane, 1.0, 0.0).astype(BF16)
            right += [z_hot, z_hot]
        acc[...] += jnp.dot(
            jnp.concatenate(left, axis=1),
            jnp.concatenate(right, axis=0),
            preferred_element_type=F32,
        )
        return 0

    lax.fori_loop(0, steps, deposit, 0)

    first_row = iota((32, DEPTH), 0) == 0
    last_row = iota((32, DEPTH), 0) == 31
    first_z = iota((32, DEPTH), 1) == 0
    last_z = iota((32, DEPTH), 1) == DEPTH - 1
    for ix in range(4):
        base = ix * 32
        volume = acc[base : base + 32, :]
        for c in range(3):
            f = fluid[c, ix]
            below = xlo[c] if ix == 0 else fluid[c, ix - 1]
            above = xhi[c] if ix == 3 else fluid[c, ix + 1]
            row = c * 4 + ix
            near = jnp.where(first_row, ylo[row : row + 1, :], pltpu.roll(f, 1, 0))
            far = jnp.where(last_row, yhi[row : row + 1, :], pltpu.roll(f, 31, 0))
            down = jnp.where(first_z, 0.0, pltpu.roll(f, 1, 1))
            up = jnp.where(last_z, 0.0, pltpu.roll(f, DEPTH - 1, 1))
            around = above + below
            around = around + far + near
            around = around + up + down
            start = (c + 1) * COLS + base
            momentum = acc[start : start + 32, :]
            value = f + viscosity * (around - 6.0 * f) + coupling * (momentum - volume * f)
            fluid_next[c, ix] = value
            high, low = split2(value)
            halves[c * COLS + base : c * COLS + base + 32, :] = high
            halves[(3 + c) * COLS + base : (3 + c) * COLS + base + 32, :] = low

    def sample(step, _):
        hots, cols = [], []
        for n in range(CHUNK):
            tile = blocks[step * CHUNK + n]
            cell = tile[4:5].astype(jnp.int32) - 1
            col, level = cell >> 9, cell & (DEPTH - 1)
            hots.append(jnp.where(z_sub == level, 1.0, 0.0).astype(BF16))
            cols.append(col_iota == col)
        along = jnp.dot(
            halves[...], jnp.concatenate(hots, axis=1), preferred_element_type=F32
        )
        for n in range(CHUNK):
            for c in range(3):
                part = along[:, n * BLK : (n + 1) * BLK]
                both = part[c * COLS : (c + 1) * COLS] + part[(3 + c) * COLS : (4 + c) * COLS]
                value = jnp.sum(jnp.where(cols[n], both, 0.0), axis=0, keepdims=True)
                sampled[step * CHUNK + n, c : c + 1, :] = value
        return 0

    lax.fori_loop(0, steps, sample, 0)
    for n in range(CAP + CHUNK):
        sampled[total + n] = blank
    for d in range(CODES):
        for k in range(CAP):
            base = d * BACK_ROWS + 3 * k
            answers[base : base + 3, :] = sampled[offset[d] + k, 0:3, :]
        answers[d * BACK_ROWS + 3 * CAP : (d + 1) * BACK_ROWS, :] = jnp.zeros(
            (BACK_ROWS - 3 * CAP, BLK), F32
        )


def advance(arrived, fluid, xlo, xhi, ylo, yhi):
    sds = jax.ShapeDtypeStruct
    room = CODES * CAP + 2 * CAP
    return pl.pallas_call(
        fluid_kernel,
        out_shape=(sds((3, 4, 32, DEPTH), F32), sds((CODES * BACK_ROWS, BLK), F32)),
        in_specs=[VMEM] * 6,
        out_specs=(VMEM,) * 2,
        scratch_shapes=[
            pltpu.VMEM((room, 8, BLK), F32),
            pltpu.VMEM((room, 8, BLK), F32),
            pltpu.VMEM((4 * COLS, DEPTH), F32),
            pltpu.VMEM((6 * COLS, DEPTH), BF16),
        ],
        compiler_params=params(48),
    )(arrived, fluid, xlo, xhi, ylo, yhi)


def on_device(
    positions, velocities, radii, cell_of, block_route, ghost_list, tile_home, tile_partner, fluid
):
    pos = jnp.transpose(positions, (1, 0, 2))
    vel = jnp.transpose(velocities, (1, 0, 2))
    route = jnp.transpose(block_route, (1, 0))
    ghosts, xlo, xhi, ylo, yhi = halo_exchange(ghost_list, pos, vel, radii, fluid)
    updated, slots, outgoing = contacts(
        tile_home, tile_partner, pos, vel, radii, cell_of, route, ghosts.reshape(32, 8, BLK)
    )
    arrived = route_blocks(outgoing)
    fluid_next, answers = advance(arrived, fluid, xlo, xhi, ylo, yhi)
    velocity_next = return_answers(slots, updated, answers)
    return jnp.transpose(velocity_next, (1, 0, 2)), fluid_next


def solution(mesh):
    placed = (
        P(("slab", "brick"), None, None),
        P(("slab", "brick"), None, None),
        P(("slab", "brick"), None),
        P(("slab", "brick"), None),
        P(("slab", "brick"), None),
        P(("slab", "brick")),
        P(("slab", "brick")),
        P(("slab", "brick")),
        P(None, "slab", "brick", None),
    )
    return jax.shard_map(
        on_device,
        mesh=mesh,
        in_specs=placed,
        out_specs=(P(("slab", "brick"), None, None), P(None, "slab", "brick", None)),
        check_vma=False,
    )
```

```python
import functools

import jax
import jax.numpy as jnp
from jax import lax
from jax.experimental import pallas as pl
from jax.experimental.pallas import tpu as pltpu
from jax.sharding import PartitionSpec as P

stiffness = 0.01
damping = 0.005
viscosity = 0.1
coupling = 0.5
relaxation = 0.5

MESH = pl.DeviceIdType.MESH
F32 = jnp.float32
BF16 = jnp.bfloat16
VMEM = pl.BlockSpec(memory_space=pltpu.VMEM)
SMEM = pl.BlockSpec(memory_space=pltpu.SMEM)
HBM = pl.BlockSpec(memory_space=pltpu.HBM)

N_SLAB = 16
N_BRICK = 8
NB = 64
BLK = 128
TILES = 128
CAND = 96
CODES = 24
CAP = 6
EARLY_ROWS = 16
LATE_ROWS = 24
BACK_ROWS = 24
COLS = 128
DEPTH = 512
BIG = 16
SMALL = 4


def iota(shape, dim, dtype=jnp.int32):
    return lax.broadcasted_iota(jnp.int32, shape, dim).astype(dtype)


def split3(x):
    high = x.astype(BF16)
    rest = x - high.astype(F32)
    middle = rest.astype(BF16)
    low = (rest - middle.astype(F32)).astype(BF16)
    return high, middle, low


def split2(x):
    high = x.astype(BF16)
    return high, (x - high.astype(F32)).astype(BF16)


def params(mib, collective_id=None):
    return pltpu.CompilerParams(
        vmem_limit_bytes=mib << 20,
        collective_id=collective_id,
        has_side_effects=collective_id is not None,
    )


def particle_kernel(
    glist_h,
    home_h,
    partner_h,
    home_v,
    pos_h,
    vel_h,
    rad_h,
    cell_h,
    route_h,
    fluid_h,
    updated,
    slots,
    early,
    late,
    xlo,
    xhi,
    ylo,
    yhi,
    glist,
    home,
    partner,
    pos,
    vel,
    rad,
    cell,
    route,
    fluid,
    gsend,
    ghosts,
    ysend,
    cand,
    jfeat,
    ifeat,
    afeat,
    terms,
    payload,
    out_early,
    out_late,
    load_sem,
    halo_send,
    halo_recv,
    early_send,
    early_recv,
    late_send,
    late_recv,
    local_sem,
):
    s, b = lax.axis_index("slab"), lax.axis_index("brick")
    upper_s = (lax.rem(s + 1, N_SLAB), b)
    lower_s = (lax.rem(s + N_SLAB - 1, N_SLAB), b)
    upper_b = (s, lax.rem(b + 1, N_BRICK))
    lower_b = (s, lax.rem(b + N_BRICK - 1, N_BRICK))
    pairs = (
        (glist_h, glist),
        (pos_h, pos),
        (vel_h, vel),
        (rad_h, rad),
        (route_h, route),
        (cell_h, cell),
        (home_h, home),
        (partner_h, partner),
        (fluid_h, fluid),
    )
    loads = [pltpu.make_async_copy(a, z, load_sem.at[n]) for n, (a, z) in enumerate(pairs)]
    for load in loads:
        load.start()
    barrier = pltpu.get_barrier_semaphore()
    greet_all(barrier)
    for load in loads[:4]:
        load.wait()
    for g in range(16):
        source = glist[g]
        i, j, k = g // 8, g // 4 % 2, g % 4
        for c in range(3):
            gsend[i, j, k, c : c + 1, :] = pos[c, pl.ds(source, 1), :]
            gsend[i, j, k, 3 + c : 4 + c, :] = vel[c, pl.ds(source, 1), :]
        gsend[i, j, k, 6:7, :] = rad[pl.ds(source, 1), :]
        gsend[i, j, k, 7:8, :] = jnp.zeros((1, BLK), F32)
    pl.semaphore_wait(barrier, 3 * N_BRICK - 1)
    plan = (
        (gsend.at[1], ghosts.at[0], upper_s),
        (gsend.at[0], ghosts.at[1], lower_s),
        (gsend.at[:, 1], ghosts.at[2], upper_b),
        (gsend.at[:, 0], ghosts.at[3], lower_b),
        (fluid.at[:, 3], xlo, upper_s),
        (fluid.at[:, 0], xhi, lower_s),
        (ysend.at[1], ylo, upper_b),
        (ysend.at[0], yhi, lower_b),
    )
    halos = [
        pltpu.make_async_remote_copy(
            src_ref=src,
            dst_ref=dst,
            send_sem=halo_send.at[n],
            recv_sem=halo_recv.at[n],
            device_id=peer,
            device_id_type=MESH,
        )
        for n, (src, dst, peer) in enumerate(plan)
    ]
    for copy in halos[:4]:
        copy.start()

    for load in loads[4:6]:
        load.wait()
    code = jnp.concatenate([route[...], route[...]], axis=1).astype(F32)
    lanes = jnp.broadcast_to(code, (BLK, BLK))
    across = jnp.transpose(lanes)
    sub, lane = iota((BLK, BLK), 0), iota((BLK, BLK), 1)
    earlier = (across == lanes) & (sub < NB) & (sub < lane % NB)
    before = jnp.sum(jnp.where(earlier, 1.0, 0.0), axis=0, keepdims=True)
    slot = (code * CAP + before).astype(jnp.int32)
    slots[...] = jnp.broadcast_to(slot, (8, BLK))
    upper_half = jnp.where(iota((1, BLK), 1) >= NB, 1, 0)

    def lay_out(channels, rows, out, per):
        groups = (len(channels) + 1) // 2
        for c, part in enumerate(channels):
            high, middle, low = split3(part)
            payload[c * NB : (c + 1) * NB, 0:BLK] = high
            payload[c * NB : (c + 1) * NB, BLK : 2 * BLK] = middle
            payload[c * NB : (c + 1) * NB, 2 * BLK : 3 * BLK] = low
        count = len(channels)
        if count % 2:
            payload[count * NB : (count + 1) * NB, :] = jnp.zeros((NB, 3 * BLK), BF16)
        key = [slot * 8 + 2 * g + upper_half for g in range(groups)]
        key = jnp.concatenate(key, axis=1) if groups > 1 else key[0]

        def piece(part, _):
            rho = iota((per, groups * BLK), 0) + part * per
            q = rho % rows
            want = ((rho // rows) * CAP + q // count) * 8 + q % count
            want = jnp.where(q < count * CAP, want, -1)
            hot = jnp.where(want == key, 1.0, 0.0).astype(BF16)
            got = jnp.dot(hot, payload[0 : groups * BLK, :], preferred_element_type=F32)
            out[pl.ds(pl.multiple_of(part * per, 8), per), :] = (
                got[:, 0:BLK] + got[:, BLK : 2 * BLK] + got[:, 2 * BLK : 3 * BLK]
            )
            return 0

        lax.fori_loop(0, CODES * rows // per, piece, 0)

    lay_out([rad[...], cell[...].astype(F32) + 1.0], EARLY_ROWS, out_early, 192)
    first = send_all(out_early, early, early_send, early_recv, local_sem.at[0], EARLY_ROWS, 1)
    for copy in first:
        copy.start()

    loads[8].wait()
    for c in range(3):
        for ix in range(4):
            at = c * 4 + ix
            ysend[0, at : at + 1, :] = fluid[c, ix, 0:1, :]
            ysend[1, at : at + 1, :] = fluid[c, ix, 31:32, :]
    for copy in halos[4:]:
        copy.start()

    for c in range(3):
        cand[0:NB, c, :] = pos[c]
        cand[0:NB, 3 + c, :] = vel[c]
    cand[0:NB, 6, :] = rad[...]
    cand[0:NB, 7, :] = jnp.zeros((NB, BLK), F32)
    row = iota((8, BLK), 0)

    def features(n, _):
        q = cand[n]
        q4 = jnp.where(row < 3, q, jnp.where(row == 3, q[6:7], 0.0))
        square = q4 * q4
        p = jnp.sum(jnp.where(row == 3, square, -square), axis=0, keepdims=True)
        jt = jnp.where(row == 4, p, jnp.where(row == 5, 1.0, q4))
        it = jnp.where(row == 5, p, jnp.where(row == 4, 1.0, 2.0 * q4))
        speed = pltpu.roll(q, 5, 0)
        at = jnp.where(
            row < 3, stiffness * q - damping * speed, jnp.where(row == 3, 1.0, 0.0)
        )
        jh, jm, jl = (x.astype(F32) for x in split3(jt))
        ih, im, il = (x.astype(F32) for x in split3(it))
        ah, am, al = (x.astype(F32) for x in split3(at))
        jfeat[n] = jnp.concatenate([jh, jh, jm, jh, jl, jm], axis=0).astype(BF16)
        ifeat[n] = jnp.concatenate([ih, im, ih, il, ih, im], axis=0).astype(BF16)
        a = jnp.concatenate([ah, am, al, jnp.zeros_like(al)], axis=0).astype(BF16)
        afeat[n] = jnp.concatenate([a, a], axis=1)
        return 0

    def features_of(step, _):
        for n in range(8):
            features(step * 8 + n, 0)
        return 0

    lax.fori_loop(0, NB // 8, features_of, 0)
    for copy in halos[:4]:
        copy.wait()
    for n in range(4):
        cand[NB + 8 * n : NB + 8 * (n + 1)] = ghosts[n].reshape(8, 8, BLK)
    lax.fori_loop(NB // 8, CAND // 8, features_of, 0)
    for load in loads[6:8]:
        load.wait()

    def tile_sum(t):
        h, p = home[t], partner[t]
        near = lax.dot_general(
            jfeat[p], ifeat[h], (((0,), (0,)), ((), ())), preferred_element_type=F32
        )
        high, low = split2(jnp.maximum(near, 0.0))
        weight = jnp.concatenate([high, low], axis=0)
        out = jnp.dot(afeat[p], weight, preferred_element_type=F32)
        return out[0:8] + out[8:16] + out[16:24]

    def tiles(step, _):
        for n, value in enumerate([tile_sum(step * 8 + n) for n in range(8)]):
            terms[step * 8 + n] = value
        return 0

    lax.fori_loop(0, TILES // 8, tiles, 0)

    belongs = jnp.where(iota((NB, TILES), 0) == home_v[...], 1.0, 0.0).astype(BF16)

    def gathered(c):
        pieces = jnp.concatenate(split3(terms[:, c, :]), axis=1)
        got = jnp.dot(belongs, pieces, preferred_element_type=F32)
        return got[:, 0:BLK] + got[:, BLK : 2 * BLK] + got[:, 2 * BLK : 3 * BLK]

    r = rad[...]
    mass = r * r * r
    weight_sum = gathered(3)
    values = []
    for c in range(3):
        a = stiffness * pos[c] - damping * vel[c]
        value = vel[c] + (a * weight_sum - gathered(c)) / mass
        updated[c] = value
        values.append(value)
    lay_out(values, LATE_ROWS, out_late, 192)
    second = send_all(out_late, late, late_send, late_recv, local_sem.at[1], LATE_ROWS, 1)
    for copy in second:
        copy.start()
    for copy in halos[4:] + first + second:
        copy.wait()


def particles(home, partner, pos, vel, rad, cell, route, glist, fluid):
    sds = jax.ShapeDtypeStruct
    return pl.pallas_call(
        particle_kernel,
        out_shape=(
            sds((3, NB, BLK), F32),
            sds((8, BLK), jnp.int32),
            sds((CODES * EARLY_ROWS, BLK), F32),
            sds((CODES * LATE_ROWS, BLK), F32),
            sds((3, 32, DEPTH), F32),
            sds((3, 32, DEPTH), F32),
            sds((16, DEPTH), F32),
            sds((16, DEPTH), F32),
        ),
        in_specs=[HBM] * 3 + [VMEM] + [HBM] * 6,
        out_specs=(VMEM,) * 8,
        scratch_shapes=[
            pltpu.SMEM((16,), jnp.int32),
            pltpu.SMEM((TILES,), jnp.int32),
            pltpu.SMEM((TILES,), jnp.int32),
            pltpu.VMEM((3, NB, BLK), F32),
            pltpu.VMEM((3, NB, BLK), F32),
            pltpu.VMEM((NB, BLK), F32),
            pltpu.VMEM((NB, BLK), jnp.int32),
            pltpu.VMEM((1, NB), jnp.int32),
            pltpu.VMEM((3, 4, 32, DEPTH), F32),
            pltpu.VMEM((2, 2, 4, 8, BLK), F32),
            pltpu.VMEM((4, 2, 4, 8, BLK), F32),
            pltpu.VMEM((2, 16, DEPTH), F32),
            pltpu.VMEM((CAND, 8, BLK), F32),
            pltpu.VMEM((CAND, 48, BLK), BF16),
            pltpu.VMEM((CAND, 48, BLK), BF16),
            pltpu.VMEM((CAND, 32, 2 * BLK), BF16),
            pltpu.VMEM((TILES, 8, BLK), F32),
            pltpu.VMEM((4 * NB, 3 * BLK), BF16),
            pltpu.VMEM((CODES * EARLY_ROWS, BLK), F32),
            pltpu.VMEM((CODES * LATE_ROWS, BLK), F32),
            pltpu.SemaphoreType.DMA((9,)),
            pltpu.SemaphoreType.DMA((8,)),
            pltpu.SemaphoreType.DMA((8,)),
            pltpu.SemaphoreType.DMA((CODES,)),
            pltpu.SemaphoreType.DMA((CODES,)),
            pltpu.SemaphoreType.DMA((CODES,)),
            pltpu.SemaphoreType.DMA((CODES,)),
            pltpu.SemaphoreType.DMA((2,)),
        ],
        compiler_params=params(40, 0),
    )(glist, home, partner, home.reshape(1, TILES), pos, vel, rad, cell, route, fluid)


def send_all(src, dst, send_sem, recv_sem, local_sem, rows, sign):
    s, b = lax.axis_index("slab"), lax.axis_index("brick")

    def region(index):
        return pl.ds(pl.multiple_of(index * rows, 8), rows)

    copies = []
    for turn in range(N_BRICK):
        brick = lax.rem(b + turn, N_BRICK)
        for o in range(3):
            slab = lax.rem(s + N_SLAB + sign * (o - 1), N_SLAB)
            n = turn * 3 + o
            source = src.at[region(o * N_BRICK + brick)]
            target = dst.at[region(o * N_BRICK + b)]
            if turn == 0 and o == 1:
                copies.append(pltpu.make_async_copy(source, target, local_sem))
            else:
                copies.append(
                    pltpu.make_async_remote_copy(
                        src_ref=source,
                        dst_ref=target,
                        send_sem=send_sem.at[n],
                        recv_sem=recv_sem.at[n],
                        device_id=(slab, brick),
                        device_id_type=MESH,
                    )
                )
    return copies


def greet_all(barrier):
    s, b = lax.axis_index("slab"), lax.axis_index("brick")
    for turn in range(N_BRICK):
        for o in range(3):
            if turn == 0 and o == 1:
                continue
            peer = (lax.rem(s + N_SLAB + o - 1, N_SLAB), lax.rem(b + turn, N_BRICK))
            pl.semaphore_signal(barrier, inc=1, device_id=peer, device_id_type=MESH)


def return_kernel(slots, updated, src, out, back, send_sem, recv_sem, local_sem):
    barrier = pltpu.get_barrier_semaphore()
    greet_all(barrier)
    pl.semaphore_wait(barrier, 3 * N_BRICK - 1)
    copies = send_all(src, back, send_sem, recv_sem, local_sem, BACK_ROWS, -1)
    for copy in copies:
        copy.start()
    for copy in copies:
        copy.wait()
    for n in range(NB):
        slot = slots[0, n]
        first = (slot // CAP) * BACK_ROWS + (slot % CAP) * 3
        for c in range(3):
            here = updated[c, n : n + 1, :]
            picked = back[pl.ds(first + c, 1), :]
            out[c, n : n + 1, :] = here + relaxation * (picked - here)


def return_answers(slots, updated, answers):
    return pl.pallas_call(
        return_kernel,
        out_shape=jax.ShapeDtypeStruct((3, NB, BLK), F32),
        in_specs=[SMEM, VMEM, VMEM],
        out_specs=VMEM,
        scratch_shapes=[
            pltpu.VMEM((CODES * BACK_ROWS, BLK), F32),
            pltpu.SemaphoreType.DMA((CODES,)),
            pltpu.SemaphoreType.DMA((CODES,)),
            pltpu.SemaphoreType.DMA,
        ],
        compiler_params=params(32, 1),
    )(slots, updated, answers)


def fluid_kernel(
    early,
    late,
    fluid_h,
    xlo,
    xhi,
    ylo,
    yhi,
    next_h,
    answers,
    fluid,
    fluid_next,
    blocks,
    sampled,
    acc,
    halves,
    load_sem,
    store_sem,
):
    load = pltpu.make_async_copy(fluid_h, fluid, load_sem)
    load.start()
    valid = jnp.zeros((CODES, 1), F32)
    for k in range(CAP):
        cells = early[pl.ds(2 * k + 1, CODES, stride=EARLY_ROWS), :]
        valid = valid + jnp.where(cells[:, 0:1] > 0.5, 1.0, 0.0)
    counted = valid.astype(jnp.int32)
    offset = []
    total = jnp.int32(0)
    for d in range(CODES):
        offset.append(total)
        total = total + counted[d, 0]
    acc[...] = jnp.zeros_like(acc)
    blank = jnp.zeros((8, BLK), F32)
    for d in range(CODES):
        for k in range(CAP):
            base = d * EARLY_ROWS + 2 * k
            blocks[offset[d] + k, 0:2, :] = early[base : base + 2, :]
            base = d * LATE_ROWS + 3 * k
            blocks[offset[d] + k, 2:5, :] = late[base : base + 3, :]
    for n in range(CAP):
        blocks[total + n] = blank
    big = total // BIG
    small = (total - big * BIG + SMALL - 1) // SMALL

    def in_chunks(run):
        def big_step(step, _):
            run(step * BIG, BIG)
            return 0

        def small_step(step, _):
            run(big * BIG + step * SMALL, SMALL)
            return 0

        lax.fori_loop(0, big, big_step, 0)
        lax.fori_loop(0, small, small_step, 0)

    col_iota = iota((COLS, BLK), 0)
    z_sub = iota((DEPTH, BLK), 0)
    z_lane = iota((BLK, DEPTH), 1)

    def deposit(first, count):
        left, right = [[], []], []
        for n in range(count):
            tile = blocks[first + n]
            cell = tile[1:2].astype(jnp.int32) - 1
            col, level = cell >> 9, cell & (DEPTH - 1)
            radius = tile[0:1]
            mass = radius * radius * radius
            hot = jnp.where(col_iota == col, 1.0, 0.0).astype(BF16)
            pieces = [split2(x) for x in [mass] + [mass * tile[2 + c : 3 + c] for c in range(3)]]
            for which in range(2):
                left[which].append(jnp.concatenate([hot * p[which] for p in pieces], axis=0))
            depth_tile = jnp.broadcast_to(level.astype(F32), (BLK, BLK))
            column = jnp.transpose(depth_tile).astype(jnp.int32)
            wide = jnp.concatenate([column] * (DEPTH // BLK), axis=1)
            right.append(jnp.where(wide == z_lane, 1.0, 0.0).astype(BF16))
        tall = jnp.concatenate([jnp.concatenate(x, axis=1) for x in left], axis=0)
        both = jnp.dot(tall, jnp.concatenate(right, axis=0), preferred_element_type=F32)
        acc[...] += both[0 : 4 * COLS] + both[4 * COLS : 8 * COLS]

    in_chunks(deposit)
    load.wait()

    first_row = iota((32, DEPTH), 0) == 0
    last_row = iota((32, DEPTH), 0) == 31
    first_z = iota((32, DEPTH), 1) == 0
    last_z = iota((32, DEPTH), 1) == DEPTH - 1
    for ix in range(4):
        base = ix * 32
        volume = acc[base : base + 32, :]
        for c in range(3):
            f = fluid[c, ix]
            below = xlo[c] if ix == 0 else fluid[c, ix - 1]
            above = xhi[c] if ix == 3 else fluid[c, ix + 1]
            row = c * 4 + ix
            near = jnp.where(first_row, ylo[row : row + 1, :], pltpu.roll(f, 1, 0))
            far = jnp.where(last_row, yhi[row : row + 1, :], pltpu.roll(f, 31, 0))
            down = jnp.where(first_z, 0.0, pltpu.roll(f, 1, 1))
            up = jnp.where(last_z, 0.0, pltpu.roll(f, DEPTH - 1, 1))
            around = above + below
            around = around + far + near
            around = around + up + down
            start = (c + 1) * COLS + base
            momentum = acc[start : start + 32, :]
            value = f + viscosity * (around - 6.0 * f) + coupling * (momentum - volume * f)
            fluid_next[c, ix] = value
            high, low = split2(value)
            halves[c * COLS + base : c * COLS + base + 32, :] = high
            halves[(3 + c) * COLS + base : (3 + c) * COLS + base + 32, :] = low
    store = pltpu.make_async_copy(fluid_next, next_h, store_sem)
    store.start()

    def sample(first, count):
        hots, cols = [], []
        for n in range(count):
            tile = blocks[first + n]
            cell = tile[1:2].astype(jnp.int32) - 1
            col, level = cell >> 9, cell & (DEPTH - 1)
            hots.append(jnp.where(z_sub == level, 1.0, 0.0).astype(BF16))
            cols.append(col_iota == col)
        along = jnp.dot(
            halves[...], jnp.concatenate(hots, axis=1), preferred_element_type=F32
        )
        for n in range(count):
            for c in range(3):
                part = along[:, n * BLK : (n + 1) * BLK]
                both = part[c * COLS : (c + 1) * COLS] + part[(3 + c) * COLS : (4 + c) * COLS]
                value = jnp.sum(jnp.where(cols[n], both, 0.0), axis=0, keepdims=True)
                sampled[first + n, c : c + 1, :] = value

    in_chunks(sample)
    for n in range(CAP):
        sampled[total + n] = blank
    for d in range(CODES):
        for k in range(CAP):
            base = d * BACK_ROWS + 3 * k
            answers[base : base + 3, :] = sampled[offset[d] + k, 0:3, :]
        answers[d * BACK_ROWS + 3 * CAP : (d + 1) * BACK_ROWS, :] = jnp.zeros(
            (BACK_ROWS - 3 * CAP, BLK), F32
        )
    store.wait()


def advance(early, late, fluid, xlo, xhi, ylo, yhi):
    sds = jax.ShapeDtypeStruct
    room = CODES * CAP + CAP + SMALL
    return pl.pallas_call(
        fluid_kernel,
        out_shape=(sds((3, 4, 32, DEPTH), F32), sds((CODES * BACK_ROWS, BLK), F32)),
        in_specs=[VMEM, VMEM, HBM] + [VMEM] * 4,
        out_specs=(HBM, VMEM),
        scratch_shapes=[
            pltpu.VMEM((3, 4, 32, DEPTH), F32),
            pltpu.VMEM((3, 4, 32, DEPTH), F32),
            pltpu.VMEM((room, 8, BLK), F32),
            pltpu.VMEM((room, 8, BLK), F32),
            pltpu.VMEM((4 * COLS, DEPTH), F32),
            pltpu.VMEM((6 * COLS, DEPTH), BF16),
            pltpu.SemaphoreType.DMA,
            pltpu.SemaphoreType.DMA,
        ],
        compiler_params=params(48),
    )(early, late, fluid, xlo, xhi, ylo, yhi)


def on_device(
    positions, velocities, radii, cell_of, block_route, ghost_list, tile_home, tile_partner, fluid
):
    pos = jnp.transpose(positions, (1, 0, 2))
    vel = jnp.transpose(velocities, (1, 0, 2))
    route = jnp.transpose(block_route, (1, 0))
    updated, slots, early, late, xlo, xhi, ylo, yhi = particles(
        tile_home, tile_partner, pos, vel, radii, cell_of, route, ghost_list, fluid
    )
    fluid_next, answers = advance(early, late, fluid, xlo, xhi, ylo, yhi)
    velocity_next = return_answers(slots, updated, answers)
    return jnp.transpose(velocity_next, (1, 0, 2)), fluid_next


def solution(mesh):
    placed = (
        P(("slab", "brick"), None, None),
        P(("slab", "brick"), None, None),
        P(("slab", "brick"), None),
        P(("slab", "brick"), None),
        P(("slab", "brick"), None),
        P(("slab", "brick")),
        P(("slab", "brick")),
        P(("slab", "brick")),
        P(None, "slab", "brick", None),
    )
    return jax.shard_map(
        on_device,
        mesh=mesh,
        in_specs=placed,
        out_specs=(P(("slab", "brick"), None, None), P(None, "slab", "brick", None)),
        check_vma=False,
    )
```

```python
import functools

import jax
import jax.numpy as jnp
from jax import lax
from jax.experimental import pallas as pl
from jax.experimental.pallas import tpu as pltpu
from jax.sharding import PartitionSpec as P

stiffness = 0.01
damping = 0.005
viscosity = 0.1
coupling = 0.5
relaxation = 0.5

MESH = pl.DeviceIdType.MESH
F32 = jnp.float32
BF16 = jnp.bfloat16
VMEM = pl.BlockSpec(memory_space=pltpu.VMEM)
SMEM = pl.BlockSpec(memory_space=pltpu.SMEM)
HBM = pl.BlockSpec(memory_space=pltpu.HBM)

N_SLAB = 16
N_BRICK = 8
NB = 64
BLK = 128
TILES = 128
CAND = 96
CODES = 24
CAP = 6
EARLY_ROWS = 12
LATE_ROWS = 18
BACK_ROWS = 18
ORDER = (4, 3, 5, 2, 6, 1, 7, 0)
COLS = 128
DEPTH = 512
BIG = 16
SMALL = 4


def iota(shape, dim, dtype=jnp.int32):
    return lax.broadcasted_iota(jnp.int32, shape, dim).astype(dtype)


def split3(x):
    high = x.astype(BF16)
    rest = x - high.astype(F32)
    middle = rest.astype(BF16)
    low = (rest - middle.astype(F32)).astype(BF16)
    return high, middle, low


def split2(x):
    high = x.astype(BF16)
    return high, (x - high.astype(F32)).astype(BF16)


def params(mib, collective_id=None):
    return pltpu.CompilerParams(
        vmem_limit_bytes=mib << 20,
        collective_id=collective_id,
        has_side_effects=collective_id is not None,
    )


def particle_kernel(
    glist_h,
    home_h,
    partner_h,
    home_row_h,
    pos_h,
    vel_h,
    rad_h,
    cell_h,
    route_h,
    fluid_h,
    updated_h,
    slots_h,
    early,
    late,
    xlo,
    xhi,
    ylo,
    yhi,
    updated,
    slots,
    glist,
    home,
    partner,
    home_row,
    pos,
    vel,
    rad,
    cell,
    route,
    fluid,
    gsend,
    ghosts,
    ysend,
    cand,
    jfeat,
    ifeat,
    afeat,
    terms,
    payload,
    out_early,
    out_late,
    load_sem,
    halo_send,
    halo_recv,
    early_send,
    early_recv,
    late_send,
    late_recv,
    local_sem,
    store_sem,
):
    s, b = lax.axis_index("slab"), lax.axis_index("brick")
    upper_s = (lax.rem(s + 1, N_SLAB), b)
    lower_s = (lax.rem(s + N_SLAB - 1, N_SLAB), b)
    upper_b = (s, lax.rem(b + 1, N_BRICK))
    lower_b = (s, lax.rem(b + N_BRICK - 1, N_BRICK))
    pairs = (
        (glist_h, glist),
        (pos_h, pos),
        (vel_h, vel),
        (rad_h, rad),
        (route_h, route),
        (cell_h, cell),
        (home_h, home),
        (partner_h, partner),
        (fluid_h, fluid),
        (home_row_h, home_row),
    )
    loads = [pltpu.make_async_copy(a, z, load_sem.at[n]) for n, (a, z) in enumerate(pairs)]
    for load in loads:
        load.start()
    barrier = pltpu.get_barrier_semaphore()
    greet_all(barrier)
    for load in loads[:4]:
        load.wait()
    for g in range(16):
        source = glist[g]
        i, j, k = g // 8, g // 4 % 2, g % 4
        for c in range(3):
            gsend[i, j, k, c : c + 1, :] = pos[c, pl.ds(source, 1), :]
            gsend[i, j, k, 3 + c : 4 + c, :] = vel[c, pl.ds(source, 1), :]
        gsend[i, j, k, 6:7, :] = rad[pl.ds(source, 1), :]
        gsend[i, j, k, 7:8, :] = jnp.zeros((1, BLK), F32)
    pl.semaphore_wait(barrier, 3 * N_BRICK - 1)
    plan = (
        (gsend.at[1], ghosts.at[0], upper_s),
        (gsend.at[0], ghosts.at[1], lower_s),
        (gsend.at[:, 1], ghosts.at[2], upper_b),
        (gsend.at[:, 0], ghosts.at[3], lower_b),
        (fluid.at[:, 3], xlo, upper_s),
        (fluid.at[:, 0], xhi, lower_s),
        (ysend.at[1], ylo, upper_b),
        (ysend.at[0], yhi, lower_b),
    )
    halos = [
        pltpu.make_async_remote_copy(
            src_ref=src,
            dst_ref=dst,
            send_sem=halo_send.at[n],
            recv_sem=halo_recv.at[n],
            device_id=peer,
            device_id_type=MESH,
        )
        for n, (src, dst, peer) in enumerate(plan)
    ]
    for copy in halos[:4]:
        copy.start()

    for load in loads[4:6]:
        load.wait()
    code = jnp.concatenate([route[...], route[...]], axis=1).astype(F32)
    lanes = jnp.broadcast_to(code, (BLK, BLK))
    across = jnp.transpose(lanes)
    sub, lane = iota((BLK, BLK), 0), iota((BLK, BLK), 1)
    earlier = (across == lanes) & (sub < NB) & (sub < lane % NB)
    before = jnp.sum(jnp.where(earlier, 1.0, 0.0), axis=0, keepdims=True)
    slot = (code * CAP + before).astype(jnp.int32)
    slots[...] = jnp.broadcast_to(slot, (8, BLK))
    keep_slots = pltpu.make_async_copy(slots, slots_h, store_sem.at[0])
    keep_slots.start()
    upper_half = jnp.where(iota((1, BLK), 1) >= NB, 1, 0)

    def lay_out(channels, rows, out):
        groups = (len(channels) + 1) // 2
        for c, part in enumerate(channels):
            high, middle, low = split3(part)
            payload[c * NB : (c + 1) * NB, 0:BLK] = high
            payload[c * NB : (c + 1) * NB, BLK : 2 * BLK] = middle
            payload[c * NB : (c + 1) * NB, 2 * BLK : 3 * BLK] = low
        count = len(channels)
        if count % 2:
            payload[count * NB : (count + 1) * NB, :] = jnp.zeros((NB, 3 * BLK), BF16)
        key = [slot * 8 + 2 * g + upper_half for g in range(groups)]
        key = jnp.concatenate(key, axis=1) if groups > 1 else key[0]

        padded = (rows + 7) // 8 * 8

        def piece(part, _):
            rho = iota((8 * padded, groups * BLK), 0)
            q = rho % padded
            want = ((part * 8 + rho // padded) * CAP + q // count) * 8 + q % count
            want = jnp.where(q < rows, want, -1)
            hot = jnp.where(want == key, 1.0, 0.0).astype(BF16)
            got = jnp.dot(hot, payload[0 : groups * BLK, :], preferred_element_type=F32)
            got = got[:, 0:BLK] + got[:, BLK : 2 * BLK] + got[:, 2 * BLK : 3 * BLK]
            out[pl.ds(part * 8, 8)] = got.reshape(8, padded, BLK)[:, 0:rows, :]
            return 0

        lax.fori_loop(0, CODES // 8, piece, 0)

    lay_out([rad[...], cell[...].astype(F32) + 1.0], EARLY_ROWS, out_early)
    first = send_all(out_early, early, early_send, early_recv, local_sem.at[0], 1)
    for copy in first:
        copy.start()

    loads[8].wait()
    for c in range(3):
        for ix in range(4):
            at = c * 4 + ix
            ysend[0, at : at + 1, :] = fluid[c, ix, 0:1, :]
            ysend[1, at : at + 1, :] = fluid[c, ix, 31:32, :]
    for copy in halos[4:]:
        copy.start()

    for c in range(3):
        cand[0:NB, c, :] = pos[c]
        cand[0:NB, 3 + c, :] = vel[c]
    cand[0:NB, 6, :] = rad[...]
    cand[0:NB, 7, :] = jnp.zeros((NB, BLK), F32)
    row = iota((8, BLK), 0)

    def features(n, _):
        q = cand[n]
        q4 = jnp.where(row < 3, q, jnp.where(row == 3, q[6:7], 0.0))
        square = q4 * q4
        p = jnp.sum(jnp.where(row == 3, square, -square), axis=0, keepdims=True)
        jt = jnp.where(row == 4, p, jnp.where(row == 5, 1.0, q4))
        it = jnp.where(row == 5, p, jnp.where(row == 4, 1.0, 2.0 * q4))
        speed = pltpu.roll(q, 5, 0)
        at = jnp.where(
            row < 3, stiffness * q - damping * speed, jnp.where(row == 3, 1.0, 0.0)
        )
        jh, jm, jl = (x.astype(F32) for x in split3(jt))
        ih, im, il = (x.astype(F32) for x in split3(it))
        ah, am, al = (x.astype(F32) for x in split3(at))
        jfeat[n] = jnp.concatenate([jh, jh, jm, jh, jl, jm], axis=0).astype(BF16)
        ifeat[n] = jnp.concatenate([ih, im, ih, il, ih, im], axis=0).astype(BF16)
        a = jnp.concatenate([ah, am, al, jnp.zeros_like(al)], axis=0).astype(BF16)
        afeat[n] = jnp.concatenate([a, a], axis=1)
        return 0

    def features_of(step, _):
        for n in range(8):
            features(step * 8 + n, 0)
        return 0

    lax.fori_loop(0, NB // 8, features_of, 0)
    for copy in halos[:4]:
        copy.wait()
    for n in range(4):
        cand[NB + 8 * n : NB + 8 * (n + 1)] = ghosts[n].reshape(8, 8, BLK)
    lax.fori_loop(NB // 8, CAND // 8, features_of, 0)
    for load in loads[6:8] + loads[9:]:
        load.wait()

    def tile_sum(t):
        h, p = home[t], partner[t]
        near = lax.dot_general(
            jfeat[p], ifeat[h], (((0,), (0,)), ((), ())), preferred_element_type=F32
        )
        high, low = split2(jnp.maximum(near, 0.0))
        weight = jnp.concatenate([high, low], axis=0)
        out = jnp.dot(afeat[p], weight, preferred_element_type=F32)
        return out[0:8] + out[8:16] + out[16:24]

    def tiles(step, _):
        for n, value in enumerate([tile_sum(step * 8 + n) for n in range(8)]):
            terms[step * 8 + n] = value
        return 0

    lax.fori_loop(0, TILES // 8, tiles, 0)

    belongs = jnp.where(iota((NB, TILES), 0) == home_row[...], 1.0, 0.0).astype(BF16)

    def gathered(c):
        pieces = jnp.concatenate(split3(terms[:, c, :]), axis=1)
        got = jnp.dot(belongs, pieces, preferred_element_type=F32)
        return got[:, 0:BLK] + got[:, BLK : 2 * BLK] + got[:, 2 * BLK : 3 * BLK]

    r = rad[...]
    mass = r * r * r
    weight_sum = gathered(3)
    values = []
    for c in range(3):
        a = stiffness * pos[c] - damping * vel[c]
        value = vel[c] + (a * weight_sum - gathered(c)) / mass
        updated[c] = value
        values.append(value)
    keep_updated = pltpu.make_async_copy(updated, updated_h, store_sem.at[1])
    keep_updated.start()
    lay_out(values, LATE_ROWS, out_late)
    second = send_all(out_late, late, late_send, late_recv, local_sem.at[1], 1)
    for copy in second:
        copy.start()
    for copy in halos[4:] + first + second + [keep_slots, keep_updated]:
        copy.wait()


def particles(home, partner, pos, vel, rad, cell, route, glist, fluid):
    sds = jax.ShapeDtypeStruct
    return pl.pallas_call(
        particle_kernel,
        out_shape=(
            sds((3, NB, BLK), F32),
            sds((8, BLK), jnp.int32),
            sds((CODES, EARLY_ROWS, BLK), F32),
            sds((CODES, LATE_ROWS, BLK), F32),
            sds((3, 32, DEPTH), F32),
            sds((3, 32, DEPTH), F32),
            sds((16, DEPTH), F32),
            sds((16, DEPTH), F32),
        ),
        in_specs=[HBM] * 10,
        out_specs=(HBM,) * 8,
        scratch_shapes=[
            pltpu.VMEM((3, NB, BLK), F32),
            pltpu.VMEM((8, BLK), jnp.int32),
            pltpu.SMEM((16,), jnp.int32),
            pltpu.SMEM((TILES,), jnp.int32),
            pltpu.SMEM((TILES,), jnp.int32),
            pltpu.VMEM((1, TILES), jnp.int32),
            pltpu.VMEM((3, NB, BLK), F32),
            pltpu.VMEM((3, NB, BLK), F32),
            pltpu.VMEM((NB, BLK), F32),
            pltpu.VMEM((NB, BLK), jnp.int32),
            pltpu.VMEM((1, NB), jnp.int32),
            pltpu.VMEM((3, 4, 32, DEPTH), F32),
            pltpu.VMEM((2, 2, 4, 8, BLK), F32),
            pltpu.VMEM((4, 2, 4, 8, BLK), F32),
            pltpu.VMEM((2, 16, DEPTH), F32),
            pltpu.VMEM((CAND, 8, BLK), F32),
            pltpu.VMEM((CAND, 48, BLK), BF16),
            pltpu.VMEM((CAND, 48, BLK), BF16),
            pltpu.VMEM((CAND, 32, 2 * BLK), BF16),
            pltpu.VMEM((TILES, 8, BLK), F32),
            pltpu.VMEM((4 * NB, 3 * BLK), BF16),
            pltpu.VMEM((CODES, EARLY_ROWS, BLK), F32),
            pltpu.VMEM((CODES, LATE_ROWS, BLK), F32),
            pltpu.SemaphoreType.DMA((10,)),
            pltpu.SemaphoreType.DMA((8,)),
            pltpu.SemaphoreType.DMA((8,)),
            pltpu.SemaphoreType.DMA((CODES,)),
            pltpu.SemaphoreType.DMA((CODES,)),
            pltpu.SemaphoreType.DMA((CODES,)),
            pltpu.SemaphoreType.DMA((CODES,)),
            pltpu.SemaphoreType.DMA((2,)),
            pltpu.SemaphoreType.DMA((2,)),
        ],
        compiler_params=params(56, 0),
    )(glist, home, partner, home.reshape(1, TILES), pos, vel, rad, cell, route, fluid)


def send_all(src, dst, send_sem, recv_sem, local_sem, sign):
    s, b = lax.axis_index("slab"), lax.axis_index("brick")
    copies = []
    for turn in ORDER:
        brick = lax.rem(b + turn, N_BRICK)
        for o in range(3):
            slab = lax.rem(s + N_SLAB + sign * (o - 1), N_SLAB)
            n = turn * 3 + o
            source = src.at[o * N_BRICK + brick]
            target = dst.at[o * N_BRICK + b]
            if turn == 0 and o == 1:
                copies.append(pltpu.make_async_copy(source, target, local_sem))
            else:
                copies.append(
                    pltpu.make_async_remote_copy(
                        src_ref=source,
                        dst_ref=target,
                        send_sem=send_sem.at[n],
                        recv_sem=recv_sem.at[n],
                        device_id=(slab, brick),
                        device_id_type=MESH,
                    )
                )
    return copies


def greet_all(barrier):
    s, b = lax.axis_index("slab"), lax.axis_index("brick")
    for turn in range(N_BRICK):
        for o in range(3):
            if turn == 0 and o == 1:
                continue
            peer = (lax.rem(s + N_SLAB + o - 1, N_SLAB), lax.rem(b + turn, N_BRICK))
            pl.semaphore_signal(barrier, inc=1, device_id=peer, device_id_type=MESH)


def return_kernel(
    slots_h, updated_h, src, out, slots, updated, back, load_sem, send_sem, recv_sem, local_sem
):
    loads = [
        pltpu.make_async_copy(slots_h.at[0], slots, load_sem.at[0]),
        pltpu.make_async_copy(updated_h, updated, load_sem.at[1]),
    ]
    for load in loads:
        load.start()
    barrier = pltpu.get_barrier_semaphore()
    greet_all(barrier)
    pl.semaphore_wait(barrier, 3 * N_BRICK - 1)
    copies = send_all(src, back, send_sem, recv_sem, local_sem, -1)
    for copy in copies:
        copy.start()
    for copy in loads + copies:
        copy.wait()
    for n in range(NB):
        slot = slots[n]
        code, first = slot // CAP, (slot % CAP) * 3
        for c in range(3):
            here = updated[c, n : n + 1, :]
            picked = back[code, pl.ds(first + c, 1), :]
            out[c, n : n + 1, :] = here + relaxation * (picked - here)


def return_answers(slots, updated, answers):
    return pl.pallas_call(
        return_kernel,
        out_shape=jax.ShapeDtypeStruct((3, NB, BLK), F32),
        in_specs=[HBM] * 3,
        out_specs=VMEM,
        scratch_shapes=[
            pltpu.SMEM((BLK,), jnp.int32),
            pltpu.VMEM((3, NB, BLK), F32),
            pltpu.VMEM((CODES, BACK_ROWS, BLK), F32),
            pltpu.SemaphoreType.DMA((2,)),
            pltpu.SemaphoreType.DMA((CODES,)),
            pltpu.SemaphoreType.DMA((CODES,)),
            pltpu.SemaphoreType.DMA,
        ],
        compiler_params=params(56, 1),
    )(slots, updated, answers)


def fluid_kernel(
    early_h,
    late_h,
    fluid_h,
    xlo_h,
    xhi_h,
    ylo_h,
    yhi_h,
    next_h,
    answers_h,
    early,
    late,
    fluid,
    xlo,
    xhi,
    ylo,
    yhi,
    answers,
    fluid_next,
    blocks,
    sampled,
    acc,
    halves,
    load_sem,
    store_sem,
):
    pairs = (
        (early_h, early),
        (late_h, late),
        (fluid_h, fluid),
        (xlo_h, xlo),
        (xhi_h, xhi),
        (ylo_h, ylo),
        (yhi_h, yhi),
    )
    loads = [pltpu.make_async_copy(a, z, load_sem.at[n]) for n, (a, z) in enumerate(pairs)]
    for load in loads:
        load.start()
    acc[...] = jnp.zeros_like(acc)
    for load in loads[:2]:
        load.wait()
    valid = jnp.zeros((CODES, 1), F32)
    for k in range(CAP):
        cells = early[:, 2 * k + 1, :]
        valid = valid + jnp.where(cells[:, 0:1] > 0.5, 1.0, 0.0)
    counted = valid.astype(jnp.int32)
    offset = []
    total = jnp.int32(0)
    for d in range(CODES):
        offset.append(total)
        total = total + counted[d, 0]
    blank = jnp.zeros((8, BLK), F32)
    for d in range(CODES):
        for k in range(CAP):
            blocks[offset[d] + k, 0:2, :] = early[d, 2 * k : 2 * k + 2, :]
            blocks[offset[d] + k, 2:5, :] = late[d, 3 * k : 3 * k + 3, :]
    for n in range(CAP):
        blocks[total + n] = blank
    big = total // BIG
    small = (total - big * BIG + SMALL - 1) // SMALL

    def in_chunks(run):
        def big_step(step, _):
            run(step * BIG, BIG)
            return 0

        def small_step(step, _):
            run(big * BIG + step * SMALL, SMALL)
            return 0

        lax.fori_loop(0, big, big_step, 0)
        lax.fori_loop(0, small, small_step, 0)

    col_iota = iota((COLS, BLK), 0)
    z_sub = iota((DEPTH, BLK), 0)
    z_lane = iota((BLK, DEPTH), 1)

    def deposit(first, count):
        left, right = [[], []], []
        for n in range(count):
            tile = blocks[first + n]
            cell = tile[1:2].astype(jnp.int32) - 1
            col, level = cell >> 9, cell & (DEPTH - 1)
            radius = tile[0:1]
            mass = radius * radius * radius
            hot = jnp.where(col_iota == col, 1.0, 0.0).astype(BF16)
            pieces = [split2(x) for x in [mass] + [mass * tile[2 + c : 3 + c] for c in range(3)]]
            for which in range(2):
                left[which].append(jnp.concatenate([hot * p[which] for p in pieces], axis=0))
            depth_tile = jnp.broadcast_to(level.astype(F32), (BLK, BLK))
            column = jnp.transpose(depth_tile).astype(jnp.int32)
            wide = jnp.concatenate([column] * (DEPTH // BLK), axis=1)
            right.append(jnp.where(wide == z_lane, 1.0, 0.0).astype(BF16))
        tall = jnp.concatenate([jnp.concatenate(x, axis=1) for x in left], axis=0)
        both = jnp.dot(tall, jnp.concatenate(right, axis=0), preferred_element_type=F32)
        acc[...] += both[0 : 4 * COLS] + both[4 * COLS : 8 * COLS]

    in_chunks(deposit)
    for load in loads[2:]:
        load.wait()

    first_row = iota((32, DEPTH), 0) == 0
    last_row = iota((32, DEPTH), 0) == 31
    first_z = iota((32, DEPTH), 1) == 0
    last_z = iota((32, DEPTH), 1) == DEPTH - 1
    for ix in range(4):
        base = ix * 32
        volume = acc[base : base + 32, :]
        for c in range(3):
            f = fluid[c, ix]
            below = xlo[c] if ix == 0 else fluid[c, ix - 1]
            above = xhi[c] if ix == 3 else fluid[c, ix + 1]
            row = c * 4 + ix
            near = jnp.where(first_row, ylo[row : row + 1, :], pltpu.roll(f, 1, 0))
            far = jnp.where(last_row, yhi[row : row + 1, :], pltpu.roll(f, 31, 0))
            down = jnp.where(first_z, 0.0, pltpu.roll(f, 1, 1))
            up = jnp.where(last_z, 0.0, pltpu.roll(f, DEPTH - 1, 1))
            around = above + below
            around = around + far + near
            around = around + up + down
            start = (c + 1) * COLS + base
            momentum = acc[start : start + 32, :]
            value = f + viscosity * (around - 6.0 * f) + coupling * (momentum - volume * f)
            fluid_next[c, ix] = value
            high, low = split2(value)
            halves[c * COLS + base : c * COLS + base + 32, :] = high
            halves[(3 + c) * COLS + base : (3 + c) * COLS + base + 32, :] = low
    store = pltpu.make_async_copy(fluid_next, next_h, store_sem)
    store.start()

    def sample(first, count):
        hots, cols = [], []
        for n in range(count):
            tile = blocks[first + n]
            cell = tile[1:2].astype(jnp.int32) - 1
            col, level = cell >> 9, cell & (DEPTH - 1)
            hots.append(jnp.where(z_sub == level, 1.0, 0.0).astype(BF16))
            cols.append(col_iota == col)
        along = jnp.dot(
            halves[...], jnp.concatenate(hots, axis=1), preferred_element_type=F32
        )
        for n in range(count):
            for c in range(3):
                part = along[:, n * BLK : (n + 1) * BLK]
                both = part[c * COLS : (c + 1) * COLS] + part[(3 + c) * COLS : (4 + c) * COLS]
                value = jnp.sum(jnp.where(cols[n], both, 0.0), axis=0, keepdims=True)
                sampled[first + n, c : c + 1, :] = value

    in_chunks(sample)
    for n in range(CAP):
        sampled[total + n] = blank
    for d in range(CODES):
        for k in range(CAP):
            answers[d, 3 * k : 3 * k + 3, :] = sampled[offset[d] + k, 0:3, :]
    back = pltpu.make_async_copy(answers, answers_h, load_sem.at[0])
    back.start()
    store.wait()
    back.wait()


def advance(early, late, fluid, xlo, xhi, ylo, yhi):
    sds = jax.ShapeDtypeStruct
    room = CODES * CAP + CAP + SMALL
    return pl.pallas_call(
        fluid_kernel,
        out_shape=(sds((3, 4, 32, DEPTH), F32), sds((CODES, BACK_ROWS, BLK), F32)),
        in_specs=[HBM] * 7,
        out_specs=(HBM, HBM),
        scratch_shapes=[
            pltpu.VMEM((CODES, EARLY_ROWS, BLK), F32),
            pltpu.VMEM((CODES, LATE_ROWS, BLK), F32),
            pltpu.VMEM((3, 4, 32, DEPTH), F32),
            pltpu.VMEM((3, 32, DEPTH), F32),
            pltpu.VMEM((3, 32, DEPTH), F32),
            pltpu.VMEM((16, DEPTH), F32),
            pltpu.VMEM((16, DEPTH), F32),
            pltpu.VMEM((CODES, BACK_ROWS, BLK), F32),
            pltpu.VMEM((3, 4, 32, DEPTH), F32),
            pltpu.VMEM((room, 8, BLK), F32),
            pltpu.VMEM((room, 8, BLK), F32),
            pltpu.VMEM((4 * COLS, DEPTH), F32),
            pltpu.VMEM((6 * COLS, DEPTH), BF16),
            pltpu.SemaphoreType.DMA((7,)),
            pltpu.SemaphoreType.DMA,
        ],
        compiler_params=params(56),
    )(early, late, fluid, xlo, xhi, ylo, yhi)


def on_device(
    positions, velocities, radii, cell_of, block_route, ghost_list, tile_home, tile_partner, fluid
):
    pos = jnp.transpose(positions, (1, 0, 2))
    vel = jnp.transpose(velocities, (1, 0, 2))
    route = jnp.transpose(block_route, (1, 0))
    updated, slots, early, late, xlo, xhi, ylo, yhi = particles(
        tile_home, tile_partner, pos, vel, radii, cell_of, route, ghost_list, fluid
    )
    fluid_next, answers = advance(early, late, fluid, xlo, xhi, ylo, yhi)
    velocity_next = return_answers(slots, updated, answers)
    return jnp.transpose(velocity_next, (1, 0, 2)), fluid_next


def solution(mesh):
    placed = (
        P(("slab", "brick"), None, None),
        P(("slab", "brick"), None, None),
        P(("slab", "brick"), None),
        P(("slab", "brick"), None),
        P(("slab", "brick"), None),
        P(("slab", "brick")),
        P(("slab", "brick")),
        P(("slab", "brick")),
        P(None, "slab", "brick", None),
    )
    return jax.shard_map(
        on_device,
        mesh=mesh,
        in_specs=placed,
        out_specs=(P(("slab", "brick"), None, None), P(None, "slab", "brick", None)),
        check_vma=False,
    )
```

```python
import functools

import jax
import jax.numpy as jnp
from jax import lax
from jax.experimental import pallas as pl
from jax.experimental.pallas import tpu as pltpu
from jax.sharding import PartitionSpec as P

stiffness = 0.01
damping = 0.005
viscosity = 0.1
coupling = 0.5
relaxation = 0.5

MESH = pl.DeviceIdType.MESH
F32 = jnp.float32
BF16 = jnp.bfloat16
VMEM = pl.BlockSpec(memory_space=pltpu.VMEM)
SMEM = pl.BlockSpec(memory_space=pltpu.SMEM)
HBM = pl.BlockSpec(memory_space=pltpu.HBM)

N_SLAB = 16
N_BRICK = 8
NB = 64
BLK = 128
TILES = 128
CAND = 96
CODES = 24
CAP = 6
EARLY_ROWS = 12
LATE_ROWS = 18
BACK_ROWS = 18
ORDER = (4, 3, 5, 2, 6, 1, 7, 0)
COLS = 128
DEPTH = 512
PER_STEP = 32
BIG = 16
SMALL = 4


def iota(shape, dim, dtype=jnp.int32):
    return lax.broadcasted_iota(jnp.int32, shape, dim).astype(dtype)


def split3(x):
    high = x.astype(BF16)
    rest = x - high.astype(F32)
    middle = rest.astype(BF16)
    low = (rest - middle.astype(F32)).astype(BF16)
    return high, middle, low


def split2(x):
    high = x.astype(BF16)
    return high, (x - high.astype(F32)).astype(BF16)


def params(mib, collective_id=None):
    return pltpu.CompilerParams(
        vmem_limit_bytes=int(mib * 1024 * 1024),
        collective_id=collective_id,
        has_side_effects=collective_id is not None,
    )


def particle_kernel(
    glist_h,
    home_h,
    partner_h,
    home_row_h,
    pos_h,
    vel_h,
    rad_h,
    cell_h,
    route_h,
    fluid_h,
    updated_h,
    slots_h,
    early,
    late,
    spread_h,
    spread,
    xlo,
    xhi,
    ylo,
    yhi,
    updated,
    slots,
    glist,
    home,
    partner,
    home_row,
    pos,
    vel,
    rad,
    cell,
    route,
    fluid,
    gsend,
    ghosts,
    ysend,
    cand,
    jfeat,
    ifeat,
    afeat,
    terms,
    payload,
    out_early,
    out_late,
    load_sem,
    halo_send,
    halo_recv,
    early_send,
    early_recv,
    late_send,
    late_recv,
    local_sem,
    store_sem,
):
    s, b = lax.axis_index("slab"), lax.axis_index("brick")
    upper_s = (lax.rem(s + 1, N_SLAB), b)
    lower_s = (lax.rem(s + N_SLAB - 1, N_SLAB), b)
    upper_b = (s, lax.rem(b + 1, N_BRICK))
    lower_b = (s, lax.rem(b + N_BRICK - 1, N_BRICK))
    pairs = (
        (glist_h, glist),
        (pos_h, pos),
        (vel_h, vel),
        (rad_h, rad),
        (route_h, route),
        (cell_h, cell),
        (home_h, home),
        (partner_h, partner),
        (fluid_h, fluid),
        (home_row_h, home_row),
    )
    loads = [pltpu.make_async_copy(a, z, load_sem.at[n]) for n, (a, z) in enumerate(pairs)]
    for load in loads:
        load.start()
    barrier = pltpu.get_barrier_semaphore()
    greet_all(barrier)
    for load in loads[:4]:
        load.wait()
    for g in range(16):
        source = glist[g]
        i, j, k = g // 8, g // 4 % 2, g % 4
        for c in range(3):
            gsend[i, j, k, c : c + 1, :] = pos[c, pl.ds(source, 1), :]
            gsend[i, j, k, 3 + c : 4 + c, :] = vel[c, pl.ds(source, 1), :]
        gsend[i, j, k, 6:7, :] = rad[pl.ds(source, 1), :]
        gsend[i, j, k, 7:8, :] = jnp.zeros((1, BLK), F32)
    pl.semaphore_wait(barrier, 3 * N_BRICK - 1)
    plan = (
        (gsend.at[1], ghosts.at[0], upper_s),
        (gsend.at[0], ghosts.at[1], lower_s),
        (gsend.at[:, 1], ghosts.at[2], upper_b),
        (gsend.at[:, 0], ghosts.at[3], lower_b),
        (fluid.at[:, 3], xlo, upper_s),
        (fluid.at[:, 0], xhi, lower_s),
        (ysend.at[1], ylo, upper_b),
        (ysend.at[0], yhi, lower_b),
    )
    halos = [
        pltpu.make_async_remote_copy(
            src_ref=src,
            dst_ref=dst,
            send_sem=halo_send.at[n],
            recv_sem=halo_recv.at[n],
            device_id=peer,
            device_id_type=MESH,
        )
        for n, (src, dst, peer) in enumerate(plan)
    ]
    for copy in halos[:4]:
        copy.start()

    for load in loads[4:6]:
        load.wait()
    code = jnp.concatenate([route[...], route[...]], axis=1).astype(F32)
    lanes = jnp.broadcast_to(code, (BLK, BLK))
    across = jnp.transpose(lanes)
    sub, lane = iota((BLK, BLK), 0), iota((BLK, BLK), 1)
    earlier = (across == lanes) & (sub < NB) & (sub < lane % NB)
    before = jnp.sum(jnp.where(earlier, 1.0, 0.0), axis=0, keepdims=True)
    slot = (code * CAP + before).astype(jnp.int32)
    slots[...] = jnp.broadcast_to(slot, (8, BLK))
    keep_slots = pltpu.make_async_copy(slots, slots_h, store_sem.at[0])
    keep_slots.start()
    upper_half = jnp.where(iota((1, BLK), 1) >= NB, 1, 0)

    def lay_out(channels, rows, out, copies):
        groups = (len(channels) + 1) // 2
        for c, part in enumerate(channels):
            high, middle, low = split3(part)
            payload[c * NB : (c + 1) * NB, 0:BLK] = high
            payload[c * NB : (c + 1) * NB, BLK : 2 * BLK] = middle
            payload[c * NB : (c + 1) * NB, 2 * BLK : 3 * BLK] = low
        count = len(channels)
        if count % 2:
            payload[count * NB : (count + 1) * NB, :] = jnp.zeros((NB, 3 * BLK), BF16)
        key = [slot * 8 + 2 * g + upper_half for g in range(groups)]
        key = jnp.concatenate(key, axis=1) if groups > 1 else key[0]

        padded = (rows + 7) // 8 * 8

        for part in range(3):
            rho = iota((8 * padded, groups * BLK), 0)
            q = rho % padded
            want = ((part * 8 + rho // padded) * CAP + q // count) * 8 + q % count
            want = jnp.where(q < rows, want, -1)
            hot = jnp.where(want == key, 1.0, 0.0).astype(BF16)
            got = jnp.dot(hot, payload[0 : groups * BLK, :], preferred_element_type=F32)
            got = got[:, 0:BLK] + got[:, BLK : 2 * BLK] + got[:, 2 * BLK : 3 * BLK]
            out[part * 8 : part * 8 + 8] = got.reshape(8, padded, BLK)[:, 0:rows, :]
        for turn in zip(*copies):
            for copy in turn:
                copy.start()

    first = send_all(out_early, early, early_send, early_recv, local_sem.at[0], 1)
    lay_out([rad[...], cell[...].astype(F32) + 1.0], EARLY_ROWS, out_early, first)

    loads[8].wait()
    for c in range(3):
        for ix in range(4):
            at = c * 4 + ix
            ysend[0, at : at + 1, :] = fluid[c, ix, 0:1, :]
            ysend[1, at : at + 1, :] = fluid[c, ix, 31:32, :]
    for copy in halos[4:]:
        copy.start()

    for c in range(3):
        cand[0:NB, c, :] = pos[c]
        cand[0:NB, 3 + c, :] = vel[c]
    cand[0:NB, 6, :] = rad[...]
    cand[0:NB, 7, :] = jnp.zeros((NB, BLK), F32)
    row = iota((8, BLK), 0)

    def features(n, _):
        q = cand[n]
        q4 = jnp.where(row < 3, q, jnp.where(row == 3, q[6:7], 0.0))
        square = q4 * q4
        p = jnp.sum(jnp.where(row == 3, square, -square), axis=0, keepdims=True)
        jt = jnp.where(row == 4, p, jnp.where(row == 5, 1.0, q4))
        it = jnp.where(row == 5, p, jnp.where(row == 4, 1.0, 2.0 * q4))
        speed = pltpu.roll(q, 5, 0)
        at = jnp.where(
            row < 3, stiffness * q - damping * speed, jnp.where(row == 3, 1.0, 0.0)
        )
        jh, jm, jl = (x.astype(F32) for x in split3(jt))
        ih, im, il = (x.astype(F32) for x in split3(it))
        ah, am, al = (x.astype(F32) for x in split3(at))
        jfeat[n] = jnp.concatenate([jh, jh, jm, jh, jl, jm], axis=0).astype(BF16)
        ifeat[n] = jnp.concatenate([ih, im, ih, il, ih, im], axis=0).astype(BF16)
        a = jnp.concatenate([ah, am, al, jnp.zeros_like(al)], axis=0).astype(BF16)
        afeat[n] = jnp.concatenate([a, a], axis=1)
        return 0

    def features_of(step, _):
        for n in range(8):
            features(step * 8 + n, 0)
        return 0

    lax.fori_loop(0, NB // 8, features_of, 0)
    for copy in halos[:4]:
        copy.wait()
    for n in range(4):
        cand[NB + 8 * n : NB + 8 * (n + 1)] = ghosts[n].reshape(8, 8, BLK)
    lax.fori_loop(NB // 8, CAND // 8, features_of, 0)
    for load in loads[6:8] + loads[9:]:
        load.wait()

    def tile_sum(t):
        h, p = home[t], partner[t]
        near = lax.dot_general(
            jfeat[p], ifeat[h], (((0,), (0,)), ((), ())), preferred_element_type=F32
        )
        high, low = split2(jnp.maximum(near, 0.0))
        weight = jnp.concatenate([high, low], axis=0)
        out = jnp.dot(afeat[p], weight, preferred_element_type=F32)
        return out[0:8] + out[8:16] + out[16:24]

    def tiles(step, _):
        first = step * PER_STEP
        for n, value in enumerate([tile_sum(first + n) for n in range(PER_STEP)]):
            terms[first + n] = value
        return 0

    lax.fori_loop(0, TILES // PER_STEP, tiles, 0)

    belongs = jnp.where(iota((NB, TILES), 0) == home_row[...], 1.0, 0.0).astype(BF16)

    def gathered(c):
        pieces = jnp.concatenate(split3(terms[:, c, :]), axis=1)
        got = jnp.dot(belongs, pieces, preferred_element_type=F32)
        return got[:, 0:BLK] + got[:, BLK : 2 * BLK] + got[:, 2 * BLK : 3 * BLK]

    r = rad[...]
    mass = r * r * r
    weight_sum = gathered(3)
    values = []
    for c in range(3):
        a = stiffness * pos[c] - damping * vel[c]
        value = vel[c] + (a * weight_sum - gathered(c)) / mass
        updated[c] = value
        values.append(value)
    keep_updated = pltpu.make_async_copy(updated, updated_h, store_sem.at[1])
    keep_updated.start()
    second = send_all(out_late, late, late_send, late_recv, local_sem.at[1], 1)
    lay_out(values, LATE_ROWS, out_late, second)

    for copy in halos[4:]:
        copy.wait()
    first_row = iota((32, DEPTH), 0) == 0
    last_row = iota((32, DEPTH), 0) == 31
    first_z = iota((32, DEPTH), 1) == 0
    last_z = iota((32, DEPTH), 1) == DEPTH - 1
    for ix in range(4):
        for c in range(3):
            f = fluid[c, ix]
            below = xlo[c] if ix == 0 else fluid[c, ix - 1]
            above = xhi[c] if ix == 3 else fluid[c, ix + 1]
            at = c * 4 + ix
            near = jnp.where(first_row, ylo[at : at + 1, :], pltpu.roll(f, 1, 0))
            far = jnp.where(last_row, yhi[at : at + 1, :], pltpu.roll(f, 31, 0))
            down = jnp.where(first_z, 0.0, pltpu.roll(f, 1, 1))
            up = jnp.where(last_z, 0.0, pltpu.roll(f, DEPTH - 1, 1))
            around = above + below
            around = around + far + near
            around = around + up + down
            spread[c, ix] = f + viscosity * (around - 6.0 * f)
    keep_spread = pltpu.make_async_copy(spread, spread_h, store_sem.at[2])
    keep_spread.start()
    for copy in sum(first + second, []) + [keep_slots, keep_updated, keep_spread]:
        copy.wait()


def particles(home, partner, pos, vel, rad, cell, route, glist, fluid):
    sds = jax.ShapeDtypeStruct
    return pl.pallas_call(
        particle_kernel,
        out_shape=(
            sds((3, NB, BLK), F32),
            sds((8, BLK), jnp.int32),
            sds((CODES, EARLY_ROWS, BLK), F32),
            sds((CODES, LATE_ROWS, BLK), F32),
            sds((3, 4, 32, DEPTH), F32),
        ),
        in_specs=[HBM] * 10,
        out_specs=(HBM,) * 5,
        scratch_shapes=[
            pltpu.VMEM((3, 4, 32, DEPTH), F32),
            pltpu.VMEM((3, 32, DEPTH), F32),
            pltpu.VMEM((3, 32, DEPTH), F32),
            pltpu.VMEM((16, DEPTH), F32),
            pltpu.VMEM((16, DEPTH), F32),
            pltpu.VMEM((3, NB, BLK), F32),
            pltpu.VMEM((8, BLK), jnp.int32),
            pltpu.SMEM((16,), jnp.int32),
            pltpu.SMEM((TILES,), jnp.int32),
            pltpu.SMEM((TILES,), jnp.int32),
            pltpu.VMEM((1, TILES), jnp.int32),
            pltpu.VMEM((3, NB, BLK), F32),
            pltpu.VMEM((3, NB, BLK), F32),
            pltpu.VMEM((NB, BLK), F32),
            pltpu.VMEM((NB, BLK), jnp.int32),
            pltpu.VMEM((1, NB), jnp.int32),
            pltpu.VMEM((3, 4, 32, DEPTH), F32),
            pltpu.VMEM((2, 2, 4, 8, BLK), F32),
            pltpu.VMEM((4, 2, 4, 8, BLK), F32),
            pltpu.VMEM((2, 16, DEPTH), F32),
            pltpu.VMEM((CAND, 8, BLK), F32),
            pltpu.VMEM((CAND, 48, BLK), BF16),
            pltpu.VMEM((CAND, 48, BLK), BF16),
            pltpu.VMEM((CAND, 32, 2 * BLK), BF16),
            pltpu.VMEM((TILES, 8, BLK), F32),
            pltpu.VMEM((4 * NB, 3 * BLK), BF16),
            pltpu.VMEM((CODES, EARLY_ROWS, BLK), F32),
            pltpu.VMEM((CODES, LATE_ROWS, BLK), F32),
            pltpu.SemaphoreType.DMA((10,)),
            pltpu.SemaphoreType.DMA((8,)),
            pltpu.SemaphoreType.DMA((8,)),
            pltpu.SemaphoreType.DMA((CODES,)),
            pltpu.SemaphoreType.DMA((CODES,)),
            pltpu.SemaphoreType.DMA((CODES,)),
            pltpu.SemaphoreType.DMA((CODES,)),
            pltpu.SemaphoreType.DMA((2,)),
            pltpu.SemaphoreType.DMA((3,)),
        ],
        compiler_params=params(56, 0),
    )(glist, home, partner, home.reshape(1, TILES), pos, vel, rad, cell, route, fluid)


def send_all(src, dst, send_sem, recv_sem, local_sem, sign):
    s, b = lax.axis_index("slab"), lax.axis_index("brick")
    copies = [[], [], []]
    for turn in ORDER:
        brick = lax.rem(b + turn, N_BRICK)
        for o in range(3):
            slab = lax.rem(s + N_SLAB + sign * (o - 1), N_SLAB)
            n = turn * 3 + o
            source = src.at[o * N_BRICK + brick]
            target = dst.at[o * N_BRICK + b]
            if turn == 0 and o == 1:
                copies[o].append(pltpu.make_async_copy(source, target, local_sem))
            else:
                copies[o].append(
                    pltpu.make_async_remote_copy(
                        src_ref=source,
                        dst_ref=target,
                        send_sem=send_sem.at[n],
                        recv_sem=recv_sem.at[n],
                        device_id=(slab, brick),
                        device_id_type=MESH,
                    )
                )
    return copies


def greet_all(barrier):
    s, b = lax.axis_index("slab"), lax.axis_index("brick")
    for turn in range(N_BRICK):
        for o in range(3):
            if turn == 0 and o == 1:
                continue
            peer = (lax.rem(s + N_SLAB + o - 1, N_SLAB), lax.rem(b + turn, N_BRICK))
            pl.semaphore_signal(barrier, inc=1, device_id=peer, device_id_type=MESH)


def return_kernel(
    slots_h, updated_h, src, out, slots, updated, back, load_sem, send_sem, recv_sem, local_sem
):
    loads = [
        pltpu.make_async_copy(slots_h.at[0], slots, load_sem.at[0]),
        pltpu.make_async_copy(updated_h, updated, load_sem.at[1]),
    ]
    for load in loads:
        load.start()
    barrier = pltpu.get_barrier_semaphore()
    greet_all(barrier)
    pl.semaphore_wait(barrier, 3 * N_BRICK - 1)
    by_offset = send_all(src, back, send_sem, recv_sem, local_sem, -1)
    copies = [copy for turn in zip(*by_offset) for copy in turn]
    for copy in copies:
        copy.start()
    for copy in loads + copies:
        copy.wait()
    for n in range(NB):
        slot = slots[n]
        code, first = slot // CAP, (slot % CAP) * 3
        for c in range(3):
            here = updated[c, n : n + 1, :]
            picked = back[code, pl.ds(first + c, 1), :]
            out[c, n : n + 1, :] = here + relaxation * (picked - here)


def return_answers(slots, updated, answers):
    return pl.pallas_call(
        return_kernel,
        out_shape=jax.ShapeDtypeStruct((3, NB, BLK), F32),
        in_specs=[HBM] * 3,
        out_specs=VMEM,
        scratch_shapes=[
            pltpu.SMEM((BLK,), jnp.int32),
            pltpu.VMEM((3, NB, BLK), F32),
            pltpu.VMEM((CODES, BACK_ROWS, BLK), F32),
            pltpu.SemaphoreType.DMA((2,)),
            pltpu.SemaphoreType.DMA((CODES,)),
            pltpu.SemaphoreType.DMA((CODES,)),
            pltpu.SemaphoreType.DMA,
        ],
        compiler_params=params(53.5, 1),
    )(slots, updated, answers)


def fluid_kernel(
    early_h,
    late_h,
    fluid_h,
    spread_h,
    next_h,
    answers_h,
    early,
    late,
    fluid,
    spread,
    answers,
    fluid_next,
    blocks,
    sampled,
    acc,
    halves,
    load_sem,
    store_sem,
):
    pairs = (
        (early_h, early),
        (late_h, late),
        (fluid_h, fluid),
        (spread_h, spread),
    )
    loads = [pltpu.make_async_copy(a, z, load_sem.at[n]) for n, (a, z) in enumerate(pairs)]
    for load in loads:
        load.start()
    acc[...] = jnp.zeros_like(acc)
    for load in loads[:2]:
        load.wait()
    valid = jnp.zeros((CODES, 1), F32)
    for k in range(CAP):
        cells = early[:, 2 * k + 1, :]
        valid = valid + jnp.where(cells[:, 0:1] > 0.5, 1.0, 0.0)
    counted = valid.astype(jnp.int32)
    offset = []
    total = jnp.int32(0)
    for d in range(CODES):
        offset.append(total)
        total = total + counted[d, 0]
    blank = jnp.zeros((8, BLK), F32)
    for d in range(CODES):
        for k in range(CAP):
            blocks[offset[d] + k, 0:2, :] = early[d, 2 * k : 2 * k + 2, :]
            blocks[offset[d] + k, 2:5, :] = late[d, 3 * k : 3 * k + 3, :]
    for n in range(CAP):
        blocks[total + n] = blank
    big = total // BIG
    small = (total - big * BIG + SMALL - 1) // SMALL

    def in_chunks(run):
        def big_step(step, _):
            run(step * BIG, BIG)
            return 0

        def small_step(step, _):
            run(big * BIG + step * SMALL, SMALL)
            return 0

        lax.fori_loop(0, big, big_step, 0)
        lax.fori_loop(0, small, small_step, 0)

    col_iota = iota((COLS, BLK), 0)
    z_sub = iota((DEPTH, BLK), 0)
    z_lane = iota((BLK, DEPTH), 1)

    def deposit(first, count):
        left, right = [[], []], []
        for n in range(count):
            tile = blocks[first + n]
            cell = tile[1:2].astype(jnp.int32) - 1
            col, level = cell >> 9, cell & (DEPTH - 1)
            radius = tile[0:1]
            mass = radius * radius * radius
            hot = jnp.where(col_iota == col, 1.0, 0.0).astype(BF16)
            pieces = [split2(x) for x in [mass] + [mass * tile[2 + c : 3 + c] for c in range(3)]]
            for which in range(2):
                left[which].append(jnp.concatenate([hot * p[which] for p in pieces], axis=0))
            depth_tile = jnp.broadcast_to(level.astype(F32), (BLK, BLK))
            column = jnp.transpose(depth_tile).astype(jnp.int32)
            wide = jnp.concatenate([column] * (DEPTH // BLK), axis=1)
            right.append(jnp.where(wide == z_lane, 1.0, 0.0).astype(BF16))
        tall = jnp.concatenate([jnp.concatenate(x, axis=1) for x in left], axis=0)
        both = jnp.dot(tall, jnp.concatenate(right, axis=0), preferred_element_type=F32)
        acc[...] += both[0 : 4 * COLS] + both[4 * COLS : 8 * COLS]

    in_chunks(deposit)
    for load in loads[2:]:
        load.wait()

    for ix in range(4):
        base = ix * 32
        volume = acc[base : base + 32, :]
        for c in range(3):
            f = fluid[c, ix]
            start = (c + 1) * COLS + base
            momentum = acc[start : start + 32, :]
            value = spread[c, ix] + coupling * (momentum - volume * f)
            fluid_next[c, ix] = value
            high, low = split2(value)
            halves[c * COLS + base : c * COLS + base + 32, :] = high
            halves[(3 + c) * COLS + base : (3 + c) * COLS + base + 32, :] = low
    store = pltpu.make_async_copy(fluid_next, next_h, store_sem)
    store.start()

    def sample(first, count):
        hots, cols = [], []
        for n in range(count):
            tile = blocks[first + n]
            cell = tile[1:2].astype(jnp.int32) - 1
            col, level = cell >> 9, cell & (DEPTH - 1)
            hots.append(jnp.where(z_sub == level, 1.0, 0.0).astype(BF16))
            cols.append(col_iota == col)
        along = jnp.dot(
            halves[...], jnp.concatenate(hots, axis=1), preferred_element_type=F32
        )
        for n in range(count):
            for c in range(3):
                part = along[:, n * BLK : (n + 1) * BLK]
                both = part[c * COLS : (c + 1) * COLS] + part[(3 + c) * COLS : (4 + c) * COLS]
                value = jnp.sum(jnp.where(cols[n], both, 0.0), axis=0, keepdims=True)
                sampled[first + n, c : c + 1, :] = value

    in_chunks(sample)
    for n in range(CAP):
        sampled[total + n] = blank
    for d in range(CODES):
        for k in range(CAP):
            answers[d, 3 * k : 3 * k + 3, :] = sampled[offset[d] + k, 0:3, :]
    back = pltpu.make_async_copy(answers, answers_h, load_sem.at[0])
    back.start()
    store.wait()
    back.wait()


def advance(early, late, fluid, spread):
    sds = jax.ShapeDtypeStruct
    room = CODES * CAP + CAP + SMALL
    return pl.pallas_call(
        fluid_kernel,
        out_shape=(sds((3, 4, 32, DEPTH), F32), sds((CODES, BACK_ROWS, BLK), F32)),
        in_specs=[HBM] * 4,
        out_specs=(HBM, HBM),
        scratch_shapes=[
            pltpu.VMEM((CODES, EARLY_ROWS, BLK), F32),
            pltpu.VMEM((CODES, LATE_ROWS, BLK), F32),
            pltpu.VMEM((3, 4, 32, DEPTH), F32),
            pltpu.VMEM((3, 4, 32, DEPTH), F32),
            pltpu.VMEM((CODES, BACK_ROWS, BLK), F32),
            pltpu.VMEM((3, 4, 32, DEPTH), F32),
            pltpu.VMEM((room, 8, BLK), F32),
            pltpu.VMEM((room, 8, BLK), F32),
            pltpu.VMEM((4 * COLS, DEPTH), F32),
            pltpu.VMEM((6 * COLS, DEPTH), BF16),
            pltpu.SemaphoreType.DMA((4,)),
            pltpu.SemaphoreType.DMA,
        ],
        compiler_params=params(56),
    )(early, late, fluid, spread)


def on_device(
    positions, velocities, radii, cell_of, block_route, ghost_list, tile_home, tile_partner, fluid
):
    pos = jnp.transpose(positions, (1, 0, 2))
    vel = jnp.transpose(velocities, (1, 0, 2))
    route = jnp.transpose(block_route, (1, 0))
    updated, slots, early, late, spread = particles(
        tile_home, tile_partner, pos, vel, radii, cell_of, route, ghost_list, fluid
    )
    fluid_next, answers = advance(early, late, fluid, spread)
    velocity_next = return_answers(slots, updated, answers)
    return jnp.transpose(velocity_next, (1, 0, 2)), fluid_next


def solution(mesh):
    placed = (
        P(("slab", "brick"), None, None),
        P(("slab", "brick"), None, None),
        P(("slab", "brick"), None),
        P(("slab", "brick"), None),
        P(("slab", "brick"), None),
        P(("slab", "brick")),
        P(("slab", "brick")),
        P(("slab", "brick")),
        P(None, "slab", "brick", None),
    )
    return jax.shard_map(
        on_device,
        mesh=mesh,
        in_specs=placed,
        out_specs=(P(("slab", "brick"), None, None), P(None, "slab", "brick", None)),
        check_vma=False,
    )
```

```python
import functools

import jax
import jax.numpy as jnp
from jax import lax
from jax.experimental import pallas as pl
from jax.experimental.pallas import tpu as pltpu
from jax.sharding import PartitionSpec as P

stiffness = 0.01
damping = 0.005
viscosity = 0.1
coupling = 0.5
relaxation = 0.5

MESH = pl.DeviceIdType.MESH
F32 = jnp.float32
BF16 = jnp.bfloat16
VMEM = pl.BlockSpec(memory_space=pltpu.VMEM)
SMEM = pl.BlockSpec(memory_space=pltpu.SMEM)
HBM = pl.BlockSpec(memory_space=pltpu.HBM)

N_SLAB = 16
N_BRICK = 8
NB = 64
BLK = 128
TILES = 128
CAND = 96
CODES = 24
CAP = 6
EARLY_ROWS = 12
LATE_ROWS = 18
BACK_ROWS = 18
ORDER = (4, 3, 5, 2, 6, 1, 7, 0)
COLS = 128
DEPTH = 512
PER_STEP = 64
BIG = 16
MIDDLE = 8
SMALL = 4


def iota(shape, dim, dtype=jnp.int32):
    return lax.broadcasted_iota(jnp.int32, shape, dim).astype(dtype)


def split3(x):
    high = x.astype(BF16)
    rest = x - high.astype(F32)
    middle = rest.astype(BF16)
    low = (rest - middle.astype(F32)).astype(BF16)
    return high, middle, low


def split2(x):
    high = x.astype(BF16)
    return high, (x - high.astype(F32)).astype(BF16)


def params(mib, collective_id=None):
    return pltpu.CompilerParams(
        vmem_limit_bytes=int(mib * 1024 * 1024),
        collective_id=collective_id,
        has_side_effects=collective_id is not None,
    )


def particle_kernel(
    glist_h,
    home_h,
    partner_h,
    home_row_h,
    pos_h,
    vel_h,
    rad_h,
    cell_h,
    route_h,
    fluid_h,
    updated_h,
    slots_h,
    early,
    late,
    spread_h,
    spread,
    xlo,
    xhi,
    ylo,
    yhi,
    updated,
    slots,
    glist,
    home,
    partner,
    home_row,
    pos,
    vel,
    rad,
    cell,
    route,
    fluid,
    gsend,
    ghosts,
    ysend,
    cand,
    jfeat,
    ifeat,
    afeat,
    terms,
    payload,
    out_early,
    out_late,
    load_sem,
    halo_send,
    halo_recv,
    early_send,
    early_recv,
    late_send,
    late_recv,
    local_sem,
    store_sem,
):
    s, b = lax.axis_index("slab"), lax.axis_index("brick")
    upper_s = (lax.rem(s + 1, N_SLAB), b)
    lower_s = (lax.rem(s + N_SLAB - 1, N_SLAB), b)
    upper_b = (s, lax.rem(b + 1, N_BRICK))
    lower_b = (s, lax.rem(b + N_BRICK - 1, N_BRICK))
    pairs = (
        (glist_h, glist),
        (pos_h, pos),
        (vel_h, vel),
        (rad_h, rad),
        (route_h, route),
        (cell_h, cell),
        (home_h, home),
        (partner_h, partner),
        (fluid_h, fluid),
        (home_row_h, home_row),
    )
    loads = [pltpu.make_async_copy(a, z, load_sem.at[n]) for n, (a, z) in enumerate(pairs)]
    for load in loads:
        load.start()
    barrier = pltpu.get_barrier_semaphore()
    greet_all(barrier)
    for load in loads[:4]:
        load.wait()
    for g in range(16):
        source = glist[g]
        i, j, k = g // 8, g // 4 % 2, g % 4
        for c in range(3):
            gsend[i, j, k, c : c + 1, :] = pos[c, pl.ds(source, 1), :]
            gsend[i, j, k, 3 + c : 4 + c, :] = vel[c, pl.ds(source, 1), :]
        gsend[i, j, k, 6:7, :] = rad[pl.ds(source, 1), :]
        gsend[i, j, k, 7:8, :] = jnp.zeros((1, BLK), F32)
    pl.semaphore_wait(barrier, 3 * N_BRICK - 1)
    plan = (
        (gsend.at[1], ghosts.at[0], upper_s),
        (gsend.at[0], ghosts.at[1], lower_s),
        (gsend.at[:, 1], ghosts.at[2], upper_b),
        (gsend.at[:, 0], ghosts.at[3], lower_b),
        (fluid.at[:, 3], xlo, upper_s),
        (fluid.at[:, 0], xhi, lower_s),
        (ysend.at[1], ylo, upper_b),
        (ysend.at[0], yhi, lower_b),
    )
    halos = [
        pltpu.make_async_remote_copy(
            src_ref=src,
            dst_ref=dst,
            send_sem=halo_send.at[n],
            recv_sem=halo_recv.at[n],
            device_id=peer,
            device_id_type=MESH,
        )
        for n, (src, dst, peer) in enumerate(plan)
    ]
    for copy in halos[:4]:
        copy.start()

    for load in loads[4:6]:
        load.wait()
    code = jnp.concatenate([route[...], route[...]], axis=1).astype(F32)
    lanes = jnp.broadcast_to(code, (BLK, BLK))
    across = jnp.transpose(lanes)
    sub, lane = iota((BLK, BLK), 0), iota((BLK, BLK), 1)
    earlier = (across == lanes) & (sub < NB) & (sub < lane % NB)
    before = jnp.sum(jnp.where(earlier, 1.0, 0.0), axis=0, keepdims=True)
    slot = (code * CAP + before).astype(jnp.int32)
    slots[...] = jnp.broadcast_to(slot, (8, BLK))
    keep_slots = pltpu.make_async_copy(slots, slots_h, store_sem.at[0])
    keep_slots.start()
    upper_half = jnp.where(iota((1, BLK), 1) >= NB, 1, 0)

    def lay_out(channels, rows, out, copies):
        groups = (len(channels) + 1) // 2
        for c, part in enumerate(channels):
            high, middle, low = split3(part)
            payload[c * NB : (c + 1) * NB, 0:BLK] = high
            payload[c * NB : (c + 1) * NB, BLK : 2 * BLK] = middle
            payload[c * NB : (c + 1) * NB, 2 * BLK : 3 * BLK] = low
        count = len(channels)
        if count % 2:
            payload[count * NB : (count + 1) * NB, :] = jnp.zeros((NB, 3 * BLK), BF16)
        key = [slot * 8 + 2 * g + upper_half for g in range(groups)]
        key = jnp.concatenate(key, axis=1) if groups > 1 else key[0]

        padded = (rows + 7) // 8 * 8

        for part in (0, 2, 1):
            rho = iota((8 * padded, groups * BLK), 0)
            q = rho % padded
            want = ((part * 8 + rho // padded) * CAP + q // count) * 8 + q % count
            want = jnp.where(q < rows, want, -1)
            hot = jnp.where(want == key, 1.0, 0.0).astype(BF16)
            got = jnp.dot(hot, payload[0 : groups * BLK, :], preferred_element_type=F32)
            got = got[:, 0:BLK] + got[:, BLK : 2 * BLK] + got[:, 2 * BLK : 3 * BLK]
            out[part * 8 : part * 8 + 8] = got.reshape(8, padded, BLK)[:, 0:rows, :]
            for copy in copies[part]:
                copy.start()

    first = send_all(out_early, early, early_send, early_recv, local_sem.at[0], 1)
    lay_out([rad[...], cell[...].astype(F32) + 1.0], EARLY_ROWS, out_early, first)

    loads[8].wait()
    for c in range(3):
        for ix in range(4):
            at = c * 4 + ix
            ysend[0, at : at + 1, :] = fluid[c, ix, 0:1, :]
            ysend[1, at : at + 1, :] = fluid[c, ix, 31:32, :]
    for copy in halos[4:]:
        copy.start()

    for c in range(3):
        cand[0:NB, c, :] = pos[c]
        cand[0:NB, 3 + c, :] = vel[c]
    cand[0:NB, 6, :] = rad[...]
    cand[0:NB, 7, :] = jnp.zeros((NB, BLK), F32)
    row = iota((8, BLK), 0)

    def features(n, _):
        q = cand[n]
        q4 = jnp.where(row < 3, q, jnp.where(row == 3, q[6:7], 0.0))
        square = q4 * q4
        p = jnp.sum(jnp.where(row == 3, square, -square), axis=0, keepdims=True)
        jt = jnp.where(row == 4, p, jnp.where(row == 5, 1.0, q4))
        it = jnp.where(row == 5, p, jnp.where(row == 4, 1.0, 2.0 * q4))
        speed = pltpu.roll(q, 5, 0)
        at = jnp.where(
            row < 3, stiffness * q - damping * speed, jnp.where(row == 3, 1.0, 0.0)
        )
        jh, jm, jl = (x.astype(F32) for x in split3(jt))
        ih, im, il = (x.astype(F32) for x in split3(it))
        ah, am, al = (x.astype(F32) for x in split3(at))
        jfeat[n] = jnp.concatenate([jh, jh, jm, jh, jl, jm], axis=0).astype(BF16)
        ifeat[n] = jnp.concatenate([ih, im, ih, il, ih, im], axis=0).astype(BF16)
        a = jnp.concatenate([ah, am, al, jnp.zeros_like(al)], axis=0).astype(BF16)
        afeat[n] = jnp.concatenate([a, a], axis=1)
        return 0

    def features_of(step, _):
        for n in range(8):
            features(step * 8 + n, 0)
        return 0

    lax.fori_loop(0, NB // 8, features_of, 0)
    for copy in halos[:4]:
        copy.wait()
    for n in range(4):
        cand[NB + 8 * n : NB + 8 * (n + 1)] = ghosts[n].reshape(8, 8, BLK)
    lax.fori_loop(NB // 8, CAND // 8, features_of, 0)
    for load in loads[6:8] + loads[9:]:
        load.wait()

    def tile_sum(t):
        h, p = home[t], partner[t]
        near = lax.dot_general(
            jfeat[p], ifeat[h], (((0,), (0,)), ((), ())), preferred_element_type=F32
        )
        high, low = split2(jnp.maximum(near, 0.0))
        weight = jnp.concatenate([high, low], axis=0)
        out = jnp.dot(afeat[p], weight, preferred_element_type=F32)
        return out[0:8] + out[8:16] + out[16:24]

    def tiles(step, _):
        first = step * PER_STEP
        for n, value in enumerate([tile_sum(first + n) for n in range(PER_STEP)]):
            terms[first + n] = value
        return 0

    lax.fori_loop(0, TILES // PER_STEP, tiles, 0)

    belongs = jnp.where(iota((NB, TILES), 0) == home_row[...], 1.0, 0.0).astype(BF16)

    def gathered(c):
        pieces = jnp.concatenate(split3(terms[:, c, :]), axis=1)
        got = jnp.dot(belongs, pieces, preferred_element_type=F32)
        return got[:, 0:BLK] + got[:, BLK : 2 * BLK] + got[:, 2 * BLK : 3 * BLK]

    r = rad[...]
    mass = r * r * r
    weight_sum = gathered(3)
    values = []
    for c in range(3):
        a = stiffness * pos[c] - damping * vel[c]
        value = vel[c] + (a * weight_sum - gathered(c)) / mass
        updated[c] = value
        values.append(value)
    keep_updated = pltpu.make_async_copy(updated, updated_h, store_sem.at[1])
    keep_updated.start()
    second = send_all(out_late, late, late_send, late_recv, local_sem.at[1], 1)
    lay_out(values, LATE_ROWS, out_late, second)

    for copy in halos[4:]:
        copy.wait()
    first_row = iota((32, DEPTH), 0) == 0
    last_row = iota((32, DEPTH), 0) == 31
    first_z = iota((32, DEPTH), 1) == 0
    last_z = iota((32, DEPTH), 1) == DEPTH - 1
    for ix in range(4):
        for c in range(3):
            f = fluid[c, ix]
            below = xlo[c] if ix == 0 else fluid[c, ix - 1]
            above = xhi[c] if ix == 3 else fluid[c, ix + 1]
            at = c * 4 + ix
            near = jnp.where(first_row, ylo[at : at + 1, :], pltpu.roll(f, 1, 0))
            far = jnp.where(last_row, yhi[at : at + 1, :], pltpu.roll(f, 31, 0))
            down = jnp.where(first_z, 0.0, pltpu.roll(f, 1, 1))
            up = jnp.where(last_z, 0.0, pltpu.roll(f, DEPTH - 1, 1))
            around = above + below
            around = around + far + near
            around = around + up + down
            spread[c, ix] = f + viscosity * (around - 6.0 * f)
    keep_spread = pltpu.make_async_copy(spread, spread_h, store_sem.at[2])
    keep_spread.start()
    for copy in sum(first + second, []) + [keep_slots, keep_updated, keep_spread]:
        copy.wait()


def particles(home, partner, pos, vel, rad, cell, route, glist, fluid):
    sds = jax.ShapeDtypeStruct
    return pl.pallas_call(
        particle_kernel,
        out_shape=(
            sds((3, NB, BLK), F32),
            sds((8, BLK), jnp.int32),
            sds((CODES, EARLY_ROWS, BLK), F32),
            sds((CODES, LATE_ROWS, BLK), F32),
            sds((3, 4, 32, DEPTH), F32),
        ),
        in_specs=[HBM] * 10,
        out_specs=(HBM,) * 5,
        scratch_shapes=[
            pltpu.VMEM((3, 4, 32, DEPTH), F32),
            pltpu.VMEM((3, 32, DEPTH), F32),
            pltpu.VMEM((3, 32, DEPTH), F32),
            pltpu.VMEM((16, DEPTH), F32),
            pltpu.VMEM((16, DEPTH), F32),
            pltpu.VMEM((3, NB, BLK), F32),
            pltpu.VMEM((8, BLK), jnp.int32),
            pltpu.SMEM((16,), jnp.int32),
            pltpu.SMEM((TILES,), jnp.int32),
            pltpu.SMEM((TILES,), jnp.int32),
            pltpu.VMEM((1, TILES), jnp.int32),
            pltpu.VMEM((3, NB, BLK), F32),
            pltpu.VMEM((3, NB, BLK), F32),
            pltpu.VMEM((NB, BLK), F32),
            pltpu.VMEM((NB, BLK), jnp.int32),
            pltpu.VMEM((1, NB), jnp.int32),
            pltpu.VMEM((3, 4, 32, DEPTH), F32),
            pltpu.VMEM((2, 2, 4, 8, BLK), F32),
            pltpu.VMEM((4, 2, 4, 8, BLK), F32),
            pltpu.VMEM((2, 16, DEPTH), F32),
            pltpu.VMEM((CAND, 8, BLK), F32),
            pltpu.VMEM((CAND, 48, BLK), BF16),
            pltpu.VMEM((CAND, 48, BLK), BF16),
            pltpu.VMEM((CAND, 32, 2 * BLK), BF16),
            pltpu.VMEM((TILES, 8, BLK), F32),
            pltpu.VMEM((4 * NB, 3 * BLK), BF16),
            pltpu.VMEM((CODES, EARLY_ROWS, BLK), F32),
            pltpu.VMEM((CODES, LATE_ROWS, BLK), F32),
            pltpu.SemaphoreType.DMA((10,)),
            pltpu.SemaphoreType.DMA((8,)),
            pltpu.SemaphoreType.DMA((8,)),
            pltpu.SemaphoreType.DMA((CODES,)),
            pltpu.SemaphoreType.DMA((CODES,)),
            pltpu.SemaphoreType.DMA((CODES,)),
            pltpu.SemaphoreType.DMA((CODES,)),
            pltpu.SemaphoreType.DMA((2,)),
            pltpu.SemaphoreType.DMA((3,)),
        ],
        compiler_params=params(56, 0),
    )(glist, home, partner, home.reshape(1, TILES), pos, vel, rad, cell, route, fluid)


def send_all(src, dst, send_sem, recv_sem, local_sem, sign):
    s, b = lax.axis_index("slab"), lax.axis_index("brick")
    copies = [[], [], []]
    for turn in ORDER:
        brick = lax.rem(b + turn, N_BRICK)
        for o in range(3):
            slab = lax.rem(s + N_SLAB + sign * (o - 1), N_SLAB)
            n = turn * 3 + o
            source = src.at[o * N_BRICK + brick]
            target = dst.at[o * N_BRICK + b]
            if turn == 0 and o == 1:
                copies[o].append(pltpu.make_async_copy(source, target, local_sem))
            else:
                copies[o].append(
                    pltpu.make_async_remote_copy(
                        src_ref=source,
                        dst_ref=target,
                        send_sem=send_sem.at[n],
                        recv_sem=recv_sem.at[n],
                        device_id=(slab, brick),
                        device_id_type=MESH,
                    )
                )
    return copies


def greet_all(barrier):
    s, b = lax.axis_index("slab"), lax.axis_index("brick")
    for turn in range(N_BRICK):
        for o in range(3):
            if turn == 0 and o == 1:
                continue
            peer = (lax.rem(s + N_SLAB + o - 1, N_SLAB), lax.rem(b + turn, N_BRICK))
            pl.semaphore_signal(barrier, inc=1, device_id=peer, device_id_type=MESH)


def return_kernel(
    slots_h, updated_h, src, out, slots, updated, back, load_sem, send_sem, recv_sem, local_sem
):
    loads = [
        pltpu.make_async_copy(slots_h.at[0], slots, load_sem.at[0]),
        pltpu.make_async_copy(updated_h, updated, load_sem.at[1]),
    ]
    for load in loads:
        load.start()
    barrier = pltpu.get_barrier_semaphore()
    greet_all(barrier)
    pl.semaphore_wait(barrier, 3 * N_BRICK - 1)
    by_offset = send_all(src, back, send_sem, recv_sem, local_sem, -1)
    copies = [copy for turn in zip(*by_offset) for copy in turn]
    for copy in copies:
        copy.start()
    for copy in loads + copies:
        copy.wait()
    for n in range(NB):
        slot = slots[n]
        code, first = slot // CAP, (slot % CAP) * 3
        for c in range(3):
            here = updated[c, n : n + 1, :]
            picked = back[code, pl.ds(first + c, 1), :]
            out[c, n : n + 1, :] = here + relaxation * (picked - here)


def return_answers(slots, updated, answers):
    return pl.pallas_call(
        return_kernel,
        out_shape=jax.ShapeDtypeStruct((3, NB, BLK), F32),
        in_specs=[HBM] * 3,
        out_specs=VMEM,
        scratch_shapes=[
            pltpu.SMEM((BLK,), jnp.int32),
            pltpu.VMEM((3, NB, BLK), F32),
            pltpu.VMEM((CODES, BACK_ROWS, BLK), F32),
            pltpu.SemaphoreType.DMA((2,)),
            pltpu.SemaphoreType.DMA((CODES,)),
            pltpu.SemaphoreType.DMA((CODES,)),
            pltpu.SemaphoreType.DMA,
        ],
        compiler_params=params(53.5, 1),
    )(slots, updated, answers)


def fluid_kernel(
    early_h,
    late_h,
    fluid_h,
    spread_h,
    next_h,
    answers_h,
    early,
    late,
    fluid,
    spread,
    answers,
    fluid_next,
    order,
    acc,
    halves,
    load_sem,
    store_sem,
):
    pairs = (
        (early_h, early.at[pl.ds(0, CODES)]),
        (late_h, late.at[pl.ds(0, CODES)]),
        (fluid_h, fluid),
        (spread_h, spread),
    )
    loads = [pltpu.make_async_copy(a, z, load_sem.at[n]) for n, (a, z) in enumerate(pairs)]
    for load in loads:
        load.start()
    acc[...] = jnp.zeros_like(acc)
    for load in loads[:2]:
        load.wait()
    valid = jnp.zeros((CODES, 1), F32)
    for k in range(CAP):
        cells = early[0:CODES, 2 * k + 1, :]
        valid = valid + jnp.where(cells[:, 0:1] > 0.5, 1.0, 0.0)
    counted = valid.astype(jnp.int32)
    offset = []
    total = jnp.int32(0)
    for d in range(CODES):
        offset.append(total)
        total = total + counted[d, 0]
    for d in range(CODES):
        for k in range(CAP):
            order[offset[d] + k] = d * 8 + k
    for n in range(SMALL):
        order[total + n] = CODES * 8
    early[CODES] = jnp.zeros((EARLY_ROWS, BLK), F32)
    late[CODES] = jnp.zeros((LATE_ROWS, BLK), F32)
    big = total // BIG
    left_over = total - big * BIG
    middle = (left_over + SMALL - 1) // MIDDLE
    left_over = jnp.maximum(left_over - middle * MIDDLE, 0)
    small = (left_over + SMALL - 1) // SMALL

    def in_chunks(run):
        def steps(count, first, size):
            def step(n, _):
                run(first + n * size, size)
                return 0

            lax.fori_loop(0, count, step, 0)

        steps(big, 0, BIG)
        steps(middle, big * BIG, MIDDLE)
        steps(small, big * BIG + middle * MIDDLE, SMALL)

    def place(n):
        at = order[n]
        return at >> 3, at & 7

    def cells_of(d, k):
        cell = early[d, pl.ds(2 * k + 1, 1), :].astype(jnp.int32) - 1
        return cell >> 9, cell & (DEPTH - 1)

    col_iota = iota((COLS, BLK), 0)
    z_sub = iota((DEPTH, BLK), 0)
    z_lane = iota((BLK, DEPTH), 1)

    def deposit(first, count):
        left, right = [[], []], []
        for n in range(count):
            d, k = place(first + n)
            col, level = cells_of(d, k)
            radius = early[d, pl.ds(2 * k, 1), :]
            mass = radius * radius * radius
            hot = jnp.where(col_iota == col, 1.0, 0.0).astype(BF16)
            pieces = [split2(x) for x in [mass] + [mass * late[d, pl.ds(3 * k + c, 1), :] for c in range(3)]]
            for which in range(2):
                left[which].append(jnp.concatenate([hot * p[which] for p in pieces], axis=0))
            depth_tile = jnp.broadcast_to(level.astype(F32), (BLK, BLK))
            column = jnp.transpose(depth_tile).astype(jnp.int32)
            wide = jnp.concatenate([column] * (DEPTH // BLK), axis=1)
            right.append(jnp.where(wide == z_lane, 1.0, 0.0).astype(BF16))
        tall = jnp.concatenate([jnp.concatenate(x, axis=1) for x in left], axis=0)
        both = jnp.dot(tall, jnp.concatenate(right, axis=0), preferred_element_type=F32)
        acc[...] += both[0 : 4 * COLS] + both[4 * COLS : 8 * COLS]

    in_chunks(deposit)
    for load in loads[2:]:
        load.wait()

    for ix in range(4):
        base = ix * 32
        volume = acc[base : base + 32, :]
        for c in range(3):
            f = fluid[c, ix]
            start = (c + 1) * COLS + base
            momentum = acc[start : start + 32, :]
            value = spread[c, ix] + coupling * (momentum - volume * f)
            fluid_next[c, ix] = value
            high, low = split2(value)
            halves[c * COLS + base : c * COLS + base + 32, :] = high
            halves[(3 + c) * COLS + base : (3 + c) * COLS + base + 32, :] = low
    store = pltpu.make_async_copy(fluid_next, next_h, store_sem)
    store.start()

    def sample(first, count):
        hots, cols = [], []
        for n in range(count):
            col, level = cells_of(*place(first + n))
            hots.append(jnp.where(z_sub == level, 1.0, 0.0).astype(BF16))
            cols.append(col_iota == col)
        along = jnp.dot(
            halves[...], jnp.concatenate(hots, axis=1), preferred_element_type=F32
        )
        for n in range(count):
            d, k = place(first + n)
            for c in range(3):
                part = along[:, n * BLK : (n + 1) * BLK]
                both = part[c * COLS : (c + 1) * COLS] + part[(3 + c) * COLS : (4 + c) * COLS]
                value = jnp.sum(jnp.where(cols[n], both, 0.0), axis=0, keepdims=True)
                answers[d, pl.ds(3 * k + c, 1), :] = value

    in_chunks(sample)
    back = pltpu.make_async_copy(answers.at[pl.ds(0, CODES)], answers_h, load_sem.at[0])
    back.start()
    store.wait()
    back.wait()


def advance(early, late, fluid, spread):
    sds = jax.ShapeDtypeStruct
    room = CODES * CAP + CAP + SMALL
    return pl.pallas_call(
        fluid_kernel,
        out_shape=(sds((3, 4, 32, DEPTH), F32), sds((CODES, BACK_ROWS, BLK), F32)),
        in_specs=[HBM] * 4,
        out_specs=(HBM, HBM),
        scratch_shapes=[
            pltpu.VMEM((CODES + 1, EARLY_ROWS, BLK), F32),
            pltpu.VMEM((CODES + 1, LATE_ROWS, BLK), F32),
            pltpu.VMEM((3, 4, 32, DEPTH), F32),
            pltpu.VMEM((3, 4, 32, DEPTH), F32),
            pltpu.VMEM((CODES + 1, BACK_ROWS, BLK), F32),
            pltpu.VMEM((3, 4, 32, DEPTH), F32),
            pltpu.SMEM((room,), jnp.int32),
            pltpu.VMEM((4 * COLS, DEPTH), F32),
            pltpu.VMEM((6 * COLS, DEPTH), BF16),
            pltpu.SemaphoreType.DMA((4,)),
            pltpu.SemaphoreType.DMA,
        ],
        compiler_params=params(56),
    )(early, late, fluid, spread)


def on_device(
    positions, velocities, radii, cell_of, block_route, ghost_list, tile_home, tile_partner, fluid
):
    pos = jnp.transpose(positions, (1, 0, 2))
    vel = jnp.transpose(velocities, (1, 0, 2))
    route = jnp.transpose(block_route, (1, 0))
    updated, slots, early, late, spread = particles(
        tile_home, tile_partner, pos, vel, radii, cell_of, route, ghost_list, fluid
    )
    fluid_next, answers = advance(early, late, fluid, spread)
    velocity_next = return_answers(slots, updated, answers)
    return jnp.transpose(velocity_next, (1, 0, 2)), fluid_next


def solution(mesh):
    placed = (
        P(("slab", "brick"), None, None),
        P(("slab", "brick"), None, None),
        P(("slab", "brick"), None),
        P(("slab", "brick"), None),
        P(("slab", "brick"), None),
        P(("slab", "brick")),
        P(("slab", "brick")),
        P(("slab", "brick")),
        P(None, "slab", "brick", None),
    )
    return jax.shard_map(
        on_device,
        mesh=mesh,
        in_specs=placed,
        out_specs=(P(("slab", "brick"), None, None), P(None, "slab", "brick", None)),
        check_vma=False,
    )
```

```python
import functools

import jax
import jax.numpy as jnp
from jax import lax
from jax.experimental import pallas as pl
from jax.experimental.pallas import tpu as pltpu
from jax.sharding import PartitionSpec as P

stiffness = 0.01
damping = 0.005
viscosity = 0.1
coupling = 0.5
relaxation = 0.5

MESH = pl.DeviceIdType.MESH
F32 = jnp.float32
BF16 = jnp.bfloat16
VMEM = pl.BlockSpec(memory_space=pltpu.VMEM)
SMEM = pl.BlockSpec(memory_space=pltpu.SMEM)
HBM = pl.BlockSpec(memory_space=pltpu.HBM)

N_SLAB = 16
N_BRICK = 8
NB = 64
BLK = 128
TILES = 128
CAND = 96
CODES = 24
CAP = 6
EARLY_ROWS = 12
LATE_ROWS = 18
BACK_ROWS = 18
ORDER = (4, 3, 5, 2, 6, 1, 7, 0)
COLS = 128
DEPTH = 512
PER_STEP = 64
CHUNKS = (32, 16, 8, 4)
SMALL = 4


def iota(shape, dim, dtype=jnp.int32):
    return lax.broadcasted_iota(jnp.int32, shape, dim).astype(dtype)


def split3(x):
    high = x.astype(BF16)
    rest = x - high.astype(F32)
    middle = rest.astype(BF16)
    low = (rest - middle.astype(F32)).astype(BF16)
    return high, middle, low


def split2(x):
    high = x.astype(BF16)
    return high, (x - high.astype(F32)).astype(BF16)


def params(mib, collective_id=None):
    return pltpu.CompilerParams(
        vmem_limit_bytes=int(mib * 1024 * 1024),
        collective_id=collective_id,
        has_side_effects=collective_id is not None,
    )


def particle_kernel(
    glist_h,
    home_h,
    partner_h,
    home_row_h,
    pos_h,
    vel_h,
    rad_h,
    cell_h,
    route_h,
    fluid_h,
    updated_h,
    slots_h,
    early,
    late,
    spread_h,
    spread,
    xlo,
    xhi,
    ylo,
    yhi,
    updated,
    slots,
    glist,
    home,
    partner,
    home_row,
    pos,
    vel,
    rad,
    cell,
    route,
    fluid,
    gsend,
    ghosts,
    ysend,
    cand,
    jfeat,
    ifeat,
    afeat,
    terms,
    payload,
    out_early,
    out_late,
    load_sem,
    halo_send,
    halo_recv,
    early_send,
    early_recv,
    late_send,
    late_recv,
    local_sem,
    store_sem,
):
    s, b = lax.axis_index("slab"), lax.axis_index("brick")
    upper_s = (lax.rem(s + 1, N_SLAB), b)
    lower_s = (lax.rem(s + N_SLAB - 1, N_SLAB), b)
    upper_b = (s, lax.rem(b + 1, N_BRICK))
    lower_b = (s, lax.rem(b + N_BRICK - 1, N_BRICK))
    pairs = (
        (glist_h, glist),
        (pos_h, pos),
        (vel_h, vel),
        (rad_h, rad),
        (route_h, route),
        (cell_h, cell),
        (home_h, home),
        (partner_h, partner),
        (fluid_h, fluid),
        (home_row_h, home_row),
    )
    loads = [pltpu.make_async_copy(a, z, load_sem.at[n]) for n, (a, z) in enumerate(pairs)]
    for load in loads:
        load.start()
    barrier = pltpu.get_barrier_semaphore()
    greet_all(barrier)
    for load in loads[:4]:
        load.wait()
    for g in range(16):
        source = glist[g]
        i, j, k = g // 8, g // 4 % 2, g % 4
        for c in range(3):
            gsend[i, j, k, c : c + 1, :] = pos[c, pl.ds(source, 1), :]
            gsend[i, j, k, 3 + c : 4 + c, :] = vel[c, pl.ds(source, 1), :]
        gsend[i, j, k, 6:7, :] = rad[pl.ds(source, 1), :]
        gsend[i, j, k, 7:8, :] = jnp.zeros((1, BLK), F32)
    pl.semaphore_wait(barrier, 3 * N_BRICK - 1)
    plan = (
        (gsend.at[1], ghosts.at[0], upper_s),
        (gsend.at[0], ghosts.at[1], lower_s),
        (gsend.at[:, 1], ghosts.at[2], upper_b),
        (gsend.at[:, 0], ghosts.at[3], lower_b),
        (fluid.at[:, 3], xlo, upper_s),
        (fluid.at[:, 0], xhi, lower_s),
        (ysend.at[1], ylo, upper_b),
        (ysend.at[0], yhi, lower_b),
    )
    halos = [
        pltpu.make_async_remote_copy(
            src_ref=src,
            dst_ref=dst,
            send_sem=halo_send.at[n],
            recv_sem=halo_recv.at[n],
            device_id=peer,
            device_id_type=MESH,
        )
        for n, (src, dst, peer) in enumerate(plan)
    ]
    for copy in halos[:4]:
        copy.start()

    for load in loads[4:6]:
        load.wait()
    code = jnp.concatenate([route[...], route[...]], axis=1).astype(F32)
    lanes = jnp.broadcast_to(code, (BLK, BLK))
    across = jnp.transpose(lanes)
    sub, lane = iota((BLK, BLK), 0), iota((BLK, BLK), 1)
    earlier = (across == lanes) & (sub < NB) & (sub < lane % NB)
    before = jnp.sum(jnp.where(earlier, 1.0, 0.0), axis=0, keepdims=True)
    slot = (code * CAP + before).astype(jnp.int32)
    slots[...] = jnp.broadcast_to(slot, (8, BLK))
    keep_slots = pltpu.make_async_copy(slots, slots_h, store_sem.at[0])
    keep_slots.start()
    upper_half = jnp.where(iota((1, BLK), 1) >= NB, 1, 0)

    def lay_out(channels, rows, out, copies):
        groups = (len(channels) + 1) // 2
        for c, part in enumerate(channels):
            high, middle, low = split3(part)
            payload[c * NB : (c + 1) * NB, 0:BLK] = high
            payload[c * NB : (c + 1) * NB, BLK : 2 * BLK] = middle
            payload[c * NB : (c + 1) * NB, 2 * BLK : 3 * BLK] = low
        count = len(channels)
        if count % 2:
            payload[count * NB : (count + 1) * NB, :] = jnp.zeros((NB, 3 * BLK), BF16)
        key = [slot * 8 + 2 * g + upper_half for g in range(groups)]
        key = jnp.concatenate(key, axis=1) if groups > 1 else key[0]

        padded = (rows + 7) // 8 * 8

        for part in (0, 2, 1):
            rho = iota((8 * padded, groups * BLK), 0)
            q = rho % padded
            want = ((part * 8 + rho // padded) * CAP + q // count) * 8 + q % count
            want = jnp.where(q < rows, want, -1)
            hot = jnp.where(want == key, 1.0, 0.0).astype(BF16)
            got = jnp.dot(hot, payload[0 : groups * BLK, :], preferred_element_type=F32)
            got = got[:, 0:BLK] + got[:, BLK : 2 * BLK] + got[:, 2 * BLK : 3 * BLK]
            out[part * 8 : part * 8 + 8] = got.reshape(8, padded, BLK)[:, 0:rows, :]
            for copy in copies[part]:
                copy.start()

    first = send_all(out_early, early, early_send, early_recv, local_sem.at[0], 1)
    lay_out([rad[...], cell[...].astype(F32) + 1.0], EARLY_ROWS, out_early, first)

    loads[8].wait()
    for c in range(3):
        for ix in range(4):
            at = c * 4 + ix
            ysend[0, at : at + 1, :] = fluid[c, ix, 0:1, :]
            ysend[1, at : at + 1, :] = fluid[c, ix, 31:32, :]
    for copy in halos[4:]:
        copy.start()

    for c in range(3):
        cand[0:NB, c, :] = pos[c]
        cand[0:NB, 3 + c, :] = vel[c]
    cand[0:NB, 6, :] = rad[...]
    cand[0:NB, 7, :] = jnp.zeros((NB, BLK), F32)
    row = iota((8, BLK), 0)

    def features(n, _):
        q = cand[n]
        q4 = jnp.where(row < 3, q, jnp.where(row == 3, q[6:7], 0.0))
        square = q4 * q4
        p = jnp.sum(jnp.where(row == 3, square, -square), axis=0, keepdims=True)
        jt = jnp.where(row == 4, p, jnp.where(row == 5, 1.0, q4))
        it = jnp.where(row == 5, p, jnp.where(row == 4, 1.0, 2.0 * q4))
        speed = pltpu.roll(q, 5, 0)
        at = jnp.where(
            row < 3, stiffness * q - damping * speed, jnp.where(row == 3, 1.0, 0.0)
        )
        jh, jm, jl = (x.astype(F32) for x in split3(jt))
        ih, im, il = (x.astype(F32) for x in split3(it))
        ah, am, al = (x.astype(F32) for x in split3(at))
        jfeat[n] = jnp.concatenate([jh, jh, jm, jh, jl, jm], axis=0).astype(BF16)
        ifeat[n] = jnp.concatenate([ih, im, ih, il, ih, im], axis=0).astype(BF16)
        a = jnp.concatenate([ah, am, al, jnp.zeros_like(al)], axis=0).astype(BF16)
        afeat[n] = jnp.concatenate([a, a], axis=1)
        return 0

    def features_of(step, _):
        for n in range(8):
            features(step * 8 + n, 0)
        return 0

    lax.fori_loop(0, NB // 8, features_of, 0)
    for copy in halos[:4]:
        copy.wait()
    for n in range(4):
        cand[NB + 8 * n : NB + 8 * (n + 1)] = ghosts[n].reshape(8, 8, BLK)
    lax.fori_loop(NB // 8, CAND // 8, features_of, 0)
    for load in loads[6:8] + loads[9:]:
        load.wait()

    def tile_sum(t):
        h, p = home[t], partner[t]
        near = lax.dot_general(
            jfeat[p], ifeat[h], (((0,), (0,)), ((), ())), preferred_element_type=F32
        )
        high, low = split2(jnp.maximum(near, 0.0))
        weight = jnp.concatenate([high, low], axis=0)
        out = jnp.dot(afeat[p], weight, preferred_element_type=F32)
        return out[0:8] + out[8:16] + out[16:24]

    def tiles(step, _):
        first = step * PER_STEP
        for n, value in enumerate([tile_sum(first + n) for n in range(PER_STEP)]):
            terms[first + n] = value
        return 0

    lax.fori_loop(0, TILES // PER_STEP, tiles, 0)

    belongs = jnp.where(iota((NB, TILES), 0) == home_row[...], 1.0, 0.0).astype(BF16)

    def gathered(c):
        pieces = jnp.concatenate(split3(terms[:, c, :]), axis=1)
        got = jnp.dot(belongs, pieces, preferred_element_type=F32)
        return got[:, 0:BLK] + got[:, BLK : 2 * BLK] + got[:, 2 * BLK : 3 * BLK]

    r = rad[...]
    mass = r * r * r
    weight_sum = gathered(3)
    values = []
    for c in range(3):
        a = stiffness * pos[c] - damping * vel[c]
        value = vel[c] + (a * weight_sum - gathered(c)) / mass
        updated[c] = value
        values.append(value)
    keep_updated = pltpu.make_async_copy(updated, updated_h, store_sem.at[1])
    keep_updated.start()
    second = send_all(out_late, late, late_send, late_recv, local_sem.at[1], 1)
    lay_out(values, LATE_ROWS, out_late, second)

    for copy in halos[4:]:
        copy.wait()
    first_row = iota((32, DEPTH), 0) == 0
    last_row = iota((32, DEPTH), 0) == 31
    first_z = iota((32, DEPTH), 1) == 0
    last_z = iota((32, DEPTH), 1) == DEPTH - 1
    for ix in range(4):
        for c in range(3):
            f = fluid[c, ix]
            below = xlo[c] if ix == 0 else fluid[c, ix - 1]
            above = xhi[c] if ix == 3 else fluid[c, ix + 1]
            at = c * 4 + ix
            near = jnp.where(first_row, ylo[at : at + 1, :], pltpu.roll(f, 1, 0))
            far = jnp.where(last_row, yhi[at : at + 1, :], pltpu.roll(f, 31, 0))
            down = jnp.where(first_z, 0.0, pltpu.roll(f, 1, 1))
            up = jnp.where(last_z, 0.0, pltpu.roll(f, DEPTH - 1, 1))
            around = above + below
            around = around + far + near
            around = around + up + down
            spread[c, ix] = f + viscosity * (around - 6.0 * f)
    keep_spread = pltpu.make_async_copy(spread, spread_h, store_sem.at[2])
    keep_spread.start()
    for copy in sum(first + second, []) + [keep_slots, keep_updated, keep_spread]:
        copy.wait()


def particles(home, partner, pos, vel, rad, cell, route, glist, fluid):
    sds = jax.ShapeDtypeStruct
    return pl.pallas_call(
        particle_kernel,
        out_shape=(
            sds((3, NB, BLK), F32),
            sds((8, BLK), jnp.int32),
            sds((CODES, EARLY_ROWS, BLK), F32),
            sds((CODES, LATE_ROWS, BLK), F32),
            sds((3, 4, 32, DEPTH), F32),
        ),
        in_specs=[HBM] * 10,
        out_specs=(HBM,) * 5,
        scratch_shapes=[
            pltpu.VMEM((3, 4, 32, DEPTH), F32),
            pltpu.VMEM((3, 32, DEPTH), F32),
            pltpu.VMEM((3, 32, DEPTH), F32),
            pltpu.VMEM((16, DEPTH), F32),
            pltpu.VMEM((16, DEPTH), F32),
            pltpu.VMEM((3, NB, BLK), F32),
            pltpu.VMEM((8, BLK), jnp.int32),
            pltpu.SMEM((16,), jnp.int32),
            pltpu.SMEM((TILES,), jnp.int32),
            pltpu.SMEM((TILES,), jnp.int32),
            pltpu.VMEM((1, TILES), jnp.int32),
            pltpu.VMEM((3, NB, BLK), F32),
            pltpu.VMEM((3, NB, BLK), F32),
            pltpu.VMEM((NB, BLK), F32),
            pltpu.VMEM((NB, BLK), jnp.int32),
            pltpu.VMEM((1, NB), jnp.int32),
            pltpu.VMEM((3, 4, 32, DEPTH), F32),
            pltpu.VMEM((2, 2, 4, 8, BLK), F32),
            pltpu.VMEM((4, 2, 4, 8, BLK), F32),
            pltpu.VMEM((2, 16, DEPTH), F32),
            pltpu.VMEM((CAND, 8, BLK), F32),
            pltpu.VMEM((CAND, 48, BLK), BF16),
            pltpu.VMEM((CAND, 48, BLK), BF16),
            pltpu.VMEM((CAND, 32, 2 * BLK), BF16),
            pltpu.VMEM((TILES, 8, BLK), F32),
            pltpu.VMEM((4 * NB, 3 * BLK), BF16),
            pltpu.VMEM((CODES, EARLY_ROWS, BLK), F32),
            pltpu.VMEM((CODES, LATE_ROWS, BLK), F32),
            pltpu.SemaphoreType.DMA((10,)),
            pltpu.SemaphoreType.DMA((8,)),
            pltpu.SemaphoreType.DMA((8,)),
            pltpu.SemaphoreType.DMA((CODES,)),
            pltpu.SemaphoreType.DMA((CODES,)),
            pltpu.SemaphoreType.DMA((CODES,)),
            pltpu.SemaphoreType.DMA((CODES,)),
            pltpu.SemaphoreType.DMA((2,)),
            pltpu.SemaphoreType.DMA((3,)),
        ],
        compiler_params=params(56, 0),
    )(glist, home, partner, home.reshape(1, TILES), pos, vel, rad, cell, route, fluid)


def send_all(src, dst, send_sem, recv_sem, local_sem, sign):
    s, b = lax.axis_index("slab"), lax.axis_index("brick")
    copies = [[], [], []]
    for turn in ORDER:
        brick = lax.rem(b + turn, N_BRICK)
        for o in range(3):
            slab = lax.rem(s + N_SLAB + sign * (o - 1), N_SLAB)
            n = turn * 3 + o
            source = src.at[o * N_BRICK + brick]
            target = dst.at[o * N_BRICK + b]
            if turn == 0 and o == 1:
                copies[o].append(pltpu.make_async_copy(source, target, local_sem))
            else:
                copies[o].append(
                    pltpu.make_async_remote_copy(
                        src_ref=source,
                        dst_ref=target,
                        send_sem=send_sem.at[n],
                        recv_sem=recv_sem.at[n],
                        device_id=(slab, brick),
                        device_id_type=MESH,
                    )
                )
    return copies


def greet_all(barrier):
    s, b = lax.axis_index("slab"), lax.axis_index("brick")
    for turn in range(N_BRICK):
        for o in range(3):
            if turn == 0 and o == 1:
                continue
            peer = (lax.rem(s + N_SLAB + o - 1, N_SLAB), lax.rem(b + turn, N_BRICK))
            pl.semaphore_signal(barrier, inc=1, device_id=peer, device_id_type=MESH)


def return_kernel(
    slots_h, updated_h, src, out, slots, updated, back, load_sem, send_sem, recv_sem, local_sem
):
    loads = [
        pltpu.make_async_copy(slots_h.at[0], slots, load_sem.at[0]),
        pltpu.make_async_copy(updated_h, updated, load_sem.at[1]),
    ]
    for load in loads:
        load.start()
    barrier = pltpu.get_barrier_semaphore()
    greet_all(barrier)
    pl.semaphore_wait(barrier, 3 * N_BRICK - 1)
    by_offset = send_all(src, back, send_sem, recv_sem, local_sem, -1)
    copies = [copy for turn in zip(*by_offset) for copy in turn]
    for copy in copies:
        copy.start()
    for copy in loads + copies:
        copy.wait()
    for n in range(NB):
        slot = slots[n]
        code, first = slot // CAP, (slot % CAP) * 3
        for c in range(3):
            here = updated[c, n : n + 1, :]
            picked = back[code, pl.ds(first + c, 1), :]
            out[c, n : n + 1, :] = here + relaxation * (picked - here)


def return_answers(slots, updated, answers):
    return pl.pallas_call(
        return_kernel,
        out_shape=jax.ShapeDtypeStruct((3, NB, BLK), F32),
        in_specs=[HBM] * 3,
        out_specs=VMEM,
        scratch_shapes=[
            pltpu.SMEM((BLK,), jnp.int32),
            pltpu.VMEM((3, NB, BLK), F32),
            pltpu.VMEM((CODES, BACK_ROWS, BLK), F32),
            pltpu.SemaphoreType.DMA((2,)),
            pltpu.SemaphoreType.DMA((CODES,)),
            pltpu.SemaphoreType.DMA((CODES,)),
            pltpu.SemaphoreType.DMA,
        ],
        compiler_params=params(53.5, 1),
    )(slots, updated, answers)


def fluid_kernel(
    early_h,
    late_h,
    fluid_h,
    spread_h,
    next_h,
    answers_h,
    early,
    late,
    fluid,
    spread,
    answers,
    fluid_next,
    order,
    acc,
    halves,
    load_sem,
    store_sem,
):
    pairs = (
        (early_h, early.at[pl.ds(0, CODES)]),
        (late_h, late.at[pl.ds(0, CODES)]),
        (fluid_h, fluid),
        (spread_h, spread),
    )
    loads = [pltpu.make_async_copy(a, z, load_sem.at[n]) for n, (a, z) in enumerate(pairs)]
    for load in loads:
        load.start()
    acc[...] = jnp.zeros_like(acc)
    for load in loads[:2]:
        load.wait()
    valid = jnp.zeros((CODES, 1), F32)
    for k in range(CAP):
        cells = early[0:CODES, 2 * k + 1, :]
        valid = valid + jnp.where(cells[:, 0:1] > 0.5, 1.0, 0.0)
    counted = valid.astype(jnp.int32)
    offset = []
    total = jnp.int32(0)
    for d in range(CODES):
        offset.append(total)
        total = total + counted[d, 0]
    for d in range(CODES):
        for k in range(CAP):
            order[offset[d] + k] = d * 8 + k
    for n in range(SMALL):
        order[total + n] = CODES * 8
    early[CODES] = jnp.zeros((EARLY_ROWS, BLK), F32)
    late[CODES] = jnp.zeros((LATE_ROWS, BLK), F32)
    counts = [total // CHUNKS[0]]
    left_over = total - counts[0] * CHUNKS[0]
    for size in CHUNKS[1:]:
        counts.append((left_over + SMALL - 1) // size)
        left_over = jnp.maximum(left_over - counts[-1] * size, 0)

    def in_chunks(run):
        first = 0
        for count, size in zip(counts, CHUNKS):

            def step(n, _):
                run(first + n * size, size)
                return 0

            lax.fori_loop(0, count, step, 0)
            first = first + count * size

    def place(n):
        at = order[n]
        return at >> 3, at & 7

    def cells_of(d, k):
        cell = early[d, pl.ds(2 * k + 1, 1), :].astype(jnp.int32) - 1
        return cell >> 9, cell & (DEPTH - 1)

    col_iota = iota((COLS, BLK), 0)
    z_sub = iota((DEPTH, BLK), 0)
    z_lane = iota((BLK, DEPTH), 1)

    def deposit(first, count):
        left, right = [[], []], []
        for n in range(count):
            d, k = place(first + n)
            col, level = cells_of(d, k)
            radius = early[d, pl.ds(2 * k, 1), :]
            mass = radius * radius * radius
            hot = jnp.where(col_iota == col, 1.0, 0.0).astype(BF16)
            pieces = [split2(x) for x in [mass] + [mass * late[d, pl.ds(3 * k + c, 1), :] for c in range(3)]]
            for which in range(2):
                left[which].append(jnp.concatenate([hot * p[which] for p in pieces], axis=0))
            depth_tile = jnp.broadcast_to(level.astype(F32), (BLK, BLK))
            column = jnp.transpose(depth_tile).astype(jnp.int32)
            wide = jnp.concatenate([column] * (DEPTH // BLK), axis=1)
            right.append(jnp.where(wide == z_lane, 1.0, 0.0).astype(BF16))
        tall = jnp.concatenate([jnp.concatenate(x, axis=1) for x in left], axis=0)
        both = jnp.dot(tall, jnp.concatenate(right, axis=0), preferred_element_type=F32)
        acc[...] += both[0 : 4 * COLS] + both[4 * COLS : 8 * COLS]

    in_chunks(deposit)
    for load in loads[2:]:
        load.wait()

    for ix in range(4):
        base = ix * 32
        volume = acc[base : base + 32, :]
        for c in range(3):
            f = fluid[c, ix]
            start = (c + 1) * COLS + base
            momentum = acc[start : start + 32, :]
            value = spread[c, ix] + coupling * (momentum - volume * f)
            fluid_next[c, ix] = value
            high, low = split2(value)
            halves[c * COLS + base : c * COLS + base + 32, :] = high
            halves[(3 + c) * COLS + base : (3 + c) * COLS + base + 32, :] = low
    store = pltpu.make_async_copy(fluid_next, next_h, store_sem)
    store.start()

    def sample(first, count):
        hots, cols = [], []
        for n in range(count):
            col, level = cells_of(*place(first + n))
            hots.append(jnp.where(z_sub == level, 1.0, 0.0).astype(BF16))
            cols.append(col_iota == col)
        along = jnp.dot(
            halves[...], jnp.concatenate(hots, axis=1), preferred_element_type=F32
        )
        for n in range(count):
            d, k = place(first + n)
            for c in range(3):
                part = along[:, n * BLK : (n + 1) * BLK]
                both = part[c * COLS : (c + 1) * COLS] + part[(3 + c) * COLS : (4 + c) * COLS]
                value = jnp.sum(jnp.where(cols[n], both, 0.0), axis=0, keepdims=True)
                answers[d, pl.ds(3 * k + c, 1), :] = value

    in_chunks(sample)
    back = pltpu.make_async_copy(answers.at[pl.ds(0, CODES)], answers_h, load_sem.at[0])
    back.start()
    store.wait()
    back.wait()


def advance(early, late, fluid, spread):
    sds = jax.ShapeDtypeStruct
    room = CODES * CAP + CAP + SMALL
    return pl.pallas_call(
        fluid_kernel,
        out_shape=(sds((3, 4, 32, DEPTH), F32), sds((CODES, BACK_ROWS, BLK), F32)),
        in_specs=[HBM] * 4,
        out_specs=(HBM, HBM),
        scratch_shapes=[
            pltpu.VMEM((CODES + 1, EARLY_ROWS, BLK), F32),
            pltpu.VMEM((CODES + 1, LATE_ROWS, BLK), F32),
            pltpu.VMEM((3, 4, 32, DEPTH), F32),
            pltpu.VMEM((3, 4, 32, DEPTH), F32),
            pltpu.VMEM((CODES + 1, BACK_ROWS, BLK), F32),
            pltpu.VMEM((3, 4, 32, DEPTH), F32),
            pltpu.SMEM((room,), jnp.int32),
            pltpu.VMEM((4 * COLS, DEPTH), F32),
            pltpu.VMEM((6 * COLS, DEPTH), BF16),
            pltpu.SemaphoreType.DMA((4,)),
            pltpu.SemaphoreType.DMA,
        ],
        compiler_params=params(56),
    )(early, late, fluid, spread)


def on_device(
    positions, velocities, radii, cell_of, block_route, ghost_list, tile_home, tile_partner, fluid
):
    pos = jnp.transpose(positions, (1, 0, 2))
    vel = jnp.transpose(velocities, (1, 0, 2))
    route = jnp.transpose(block_route, (1, 0))
    updated, slots, early, late, spread = particles(
        tile_home, tile_partner, pos, vel, radii, cell_of, route, ghost_list, fluid
    )
    fluid_next, answers = advance(early, late, fluid, spread)
    velocity_next = return_answers(slots, updated, answers)
    return jnp.transpose(velocity_next, (1, 0, 2)), fluid_next


def solution(mesh):
    placed = (
        P(("slab", "brick"), None, None),
        P(("slab", "brick"), None, None),
        P(("slab", "brick"), None),
        P(("slab", "brick"), None),
        P(("slab", "brick"), None),
        P(("slab", "brick")),
        P(("slab", "brick")),
        P(("slab", "brick")),
        P(None, "slab", "brick", None),
    )
    return jax.shard_map(
        on_device,
        mesh=mesh,
        in_specs=placed,
        out_specs=(P(("slab", "brick"), None, None), P(None, "slab", "brick", None)),
        check_vma=False,
    )
```

```python
import functools

import jax
import jax.numpy as jnp
from jax import lax
from jax.experimental import pallas as pl
from jax.experimental.pallas import tpu as pltpu
from jax.sharding import PartitionSpec as P

stiffness = 0.01
damping = 0.005
viscosity = 0.1
coupling = 0.5
relaxation = 0.5

MESH = pl.DeviceIdType.MESH
F32 = jnp.float32
BF16 = jnp.bfloat16
VMEM = pl.BlockSpec(memory_space=pltpu.VMEM)
SMEM = pl.BlockSpec(memory_space=pltpu.SMEM)
HBM = pl.BlockSpec(memory_space=pltpu.HBM)

N_SLAB = 16
N_BRICK = 8
NB = 64
BLK = 128
TILES = 128
CAND = 96
CODES = 24
CAP = 6
EARLY_ROWS = 12
LATE_ROWS = 18
BACK_ROWS = 18
ORDER = (4, 3, 5, 2, 6, 1, 7, 0)
COLS = 128
DEPTH = 512
PER_STEP = 128
CHUNKS = (48, 16, 8, 4)
SMALL = 4


def iota(shape, dim, dtype=jnp.int32):
    return lax.broadcasted_iota(jnp.int32, shape, dim).astype(dtype)


def split3(x):
    high = x.astype(BF16)
    rest = x - high.astype(F32)
    middle = rest.astype(BF16)
    low = (rest - middle.astype(F32)).astype(BF16)
    return high, middle, low


def split2(x):
    high = x.astype(BF16)
    return high, (x - high.astype(F32)).astype(BF16)


def params(mib, collective_id=None):
    return pltpu.CompilerParams(
        vmem_limit_bytes=int(mib * 1024 * 1024),
        collective_id=collective_id,
        has_side_effects=collective_id is not None,
    )


def particle_kernel(
    glist_h,
    home_h,
    partner_h,
    home_row_h,
    pos_h,
    vel_h,
    rad_h,
    cell_h,
    route_h,
    fluid_h,
    updated_h,
    slots_h,
    early,
    late,
    spread_h,
    spread,
    xlo,
    xhi,
    ylo,
    yhi,
    updated,
    slots,
    glist,
    home,
    partner,
    home_row,
    pos,
    vel,
    rad,
    cell,
    route,
    fluid,
    gsend,
    ghosts,
    ysend,
    cand,
    jfeat,
    ifeat,
    afeat,
    terms,
    payload,
    out_early,
    out_late,
    load_sem,
    halo_send,
    halo_recv,
    early_send,
    early_recv,
    late_send,
    late_recv,
    local_sem,
    store_sem,
):
    s, b = lax.axis_index("slab"), lax.axis_index("brick")
    upper_s = (lax.rem(s + 1, N_SLAB), b)
    lower_s = (lax.rem(s + N_SLAB - 1, N_SLAB), b)
    upper_b = (s, lax.rem(b + 1, N_BRICK))
    lower_b = (s, lax.rem(b + N_BRICK - 1, N_BRICK))
    pairs = (
        (glist_h, glist),
        (pos_h, pos),
        (vel_h, vel),
        (rad_h, rad),
        (route_h, route),
        (cell_h, cell),
        (home_h, home),
        (partner_h, partner),
        (fluid_h, fluid),
        (home_row_h, home_row),
    )
    loads = [pltpu.make_async_copy(a, z, load_sem.at[n]) for n, (a, z) in enumerate(pairs)]
    for load in loads:
        load.start()
    barrier = pltpu.get_barrier_semaphore()
    greet_all(barrier)
    for load in loads[:4]:
        load.wait()
    for g in range(16):
        source = glist[g]
        i, j, k = g // 8, g // 4 % 2, g % 4
        for c in range(3):
            gsend[i, j, k, c : c + 1, :] = pos[c, pl.ds(source, 1), :]
            gsend[i, j, k, 3 + c : 4 + c, :] = vel[c, pl.ds(source, 1), :]
        gsend[i, j, k, 6:7, :] = rad[pl.ds(source, 1), :]
        gsend[i, j, k, 7:8, :] = jnp.zeros((1, BLK), F32)
    pl.semaphore_wait(barrier, 3 * N_BRICK - 1)
    plan = (
        (gsend.at[1], ghosts.at[0], upper_s),
        (gsend.at[0], ghosts.at[1], lower_s),
        (gsend.at[:, 1], ghosts.at[2], upper_b),
        (gsend.at[:, 0], ghosts.at[3], lower_b),
        (fluid.at[:, 3], xlo, upper_s),
        (fluid.at[:, 0], xhi, lower_s),
        (ysend.at[1], ylo, upper_b),
        (ysend.at[0], yhi, lower_b),
    )
    halos = [
        pltpu.make_async_remote_copy(
            src_ref=src,
            dst_ref=dst,
            send_sem=halo_send.at[n],
            recv_sem=halo_recv.at[n],
            device_id=peer,
            device_id_type=MESH,
        )
        for n, (src, dst, peer) in enumerate(plan)
    ]
    for copy in halos[:4]:
        copy.start()

    for load in loads[4:6]:
        load.wait()
    code = jnp.concatenate([route[...], route[...]], axis=1).astype(F32)
    lanes = jnp.broadcast_to(code, (BLK, BLK))
    across = jnp.transpose(lanes)
    sub, lane = iota((BLK, BLK), 0), iota((BLK, BLK), 1)
    earlier = (across == lanes) & (sub < NB) & (sub < lane % NB)
    before = jnp.sum(jnp.where(earlier, 1.0, 0.0), axis=0, keepdims=True)
    slot = (code * CAP + before).astype(jnp.int32)
    slots[...] = jnp.broadcast_to(slot, (8, BLK))
    keep_slots = pltpu.make_async_copy(slots, slots_h, store_sem.at[0])
    keep_slots.start()
    upper_half = jnp.where(iota((1, BLK), 1) >= NB, 1, 0)

    def lay_out(channels, rows, out, copies):
        groups = (len(channels) + 1) // 2
        for c, part in enumerate(channels):
            high, middle, low = split3(part)
            payload[c * NB : (c + 1) * NB, 0:BLK] = high
            payload[c * NB : (c + 1) * NB, BLK : 2 * BLK] = middle
            payload[c * NB : (c + 1) * NB, 2 * BLK : 3 * BLK] = low
        count = len(channels)
        if count % 2:
            payload[count * NB : (count + 1) * NB, :] = jnp.zeros((NB, 3 * BLK), BF16)
        key = [slot * 8 + 2 * g + upper_half for g in range(groups)]
        key = jnp.concatenate(key, axis=1) if groups > 1 else key[0]

        padded = (rows + 7) // 8 * 8

        for part in (0, 2, 1):
            rho = iota((8 * padded, groups * BLK), 0)
            q = rho % padded
            want = ((part * 8 + rho // padded) * CAP + q // count) * 8 + q % count
            want = jnp.where(q < rows, want, -1)
            hot = jnp.where(want == key, 1.0, 0.0).astype(BF16)
            got = jnp.dot(hot, payload[0 : groups * BLK, :], preferred_element_type=F32)
            got = got[:, 0:BLK] + got[:, BLK : 2 * BLK] + got[:, 2 * BLK : 3 * BLK]
            out[part * 8 : part * 8 + 8] = got.reshape(8, padded, BLK)[:, 0:rows, :]
            for copy in copies[part]:
                copy.start()

    first = send_all(out_early, early, early_send, early_recv, local_sem.at[0], 1)
    lay_out([rad[...], cell[...].astype(F32) + 1.0], EARLY_ROWS, out_early, first)

    loads[8].wait()
    for c in range(3):
        for ix in range(4):
            at = c * 4 + ix
            ysend[0, at : at + 1, :] = fluid[c, ix, 0:1, :]
            ysend[1, at : at + 1, :] = fluid[c, ix, 31:32, :]
    for copy in halos[4:]:
        copy.start()

    for c in range(3):
        cand[0:NB, c, :] = pos[c]
        cand[0:NB, 3 + c, :] = vel[c]
    cand[0:NB, 6, :] = rad[...]
    cand[0:NB, 7, :] = jnp.zeros((NB, BLK), F32)
    row = iota((8, BLK), 0)

    def features(n, _):
        q = cand[n]
        q4 = jnp.where(row < 3, q, jnp.where(row == 3, q[6:7], 0.0))
        square = q4 * q4
        p = jnp.sum(jnp.where(row == 3, square, -square), axis=0, keepdims=True)
        jt = jnp.where(row == 4, p, jnp.where(row == 5, 1.0, q4))
        it = jnp.where(row == 5, p, jnp.where(row == 4, 1.0, 2.0 * q4))
        speed = pltpu.roll(q, 5, 0)
        at = jnp.where(
            row < 3, stiffness * q - damping * speed, jnp.where(row == 3, 1.0, 0.0)
        )
        jh, jm, jl = (x.astype(F32) for x in split3(jt))
        ih, im, il = (x.astype(F32) for x in split3(it))
        ah, am, al = (x.astype(F32) for x in split3(at))
        jfeat[n] = jnp.concatenate([jh, jh, jm, jh, jl, jm], axis=0).astype(BF16)
        ifeat[n] = jnp.concatenate([ih, im, ih, il, ih, im], axis=0).astype(BF16)
        a = jnp.concatenate([ah, am, al, jnp.zeros_like(al)], axis=0).astype(BF16)
        afeat[n] = jnp.concatenate([a, a], axis=1)
        return 0

    def features_of(step, _):
        for n in range(8):
            features(step * 8 + n, 0)
        return 0

    lax.fori_loop(0, NB // 8, features_of, 0)
    for copy in halos[:4]:
        copy.wait()
    for n in range(4):
        cand[NB + 8 * n : NB + 8 * (n + 1)] = ghosts[n].reshape(8, 8, BLK)
    lax.fori_loop(NB // 8, CAND // 8, features_of, 0)
    for load in loads[6:8] + loads[9:]:
        load.wait()

    def tile_sum(t):
        h, p = home[t], partner[t]
        near = lax.dot_general(
            jfeat[p], ifeat[h], (((0,), (0,)), ((), ())), preferred_element_type=F32
        )
        high, low = split2(jnp.maximum(near, 0.0))
        weight = jnp.concatenate([high, low], axis=0)
        out = jnp.dot(afeat[p], weight, preferred_element_type=F32)
        return out[0:8] + out[8:16] + out[16:24]

    def tiles(step, _):
        first = step * PER_STEP
        for n, value in enumerate([tile_sum(first + n) for n in range(PER_STEP)]):
            terms[first + n] = value
        return 0

    lax.fori_loop(0, TILES // PER_STEP, tiles, 0)

    belongs = jnp.where(iota((NB, TILES), 0) == home_row[...], 1.0, 0.0).astype(BF16)

    def gathered(c):
        pieces = jnp.concatenate(split3(terms[:, c, :]), axis=1)
        got = jnp.dot(belongs, pieces, preferred_element_type=F32)
        return got[:, 0:BLK] + got[:, BLK : 2 * BLK] + got[:, 2 * BLK : 3 * BLK]

    r = rad[...]
    mass = r * r * r
    weight_sum = gathered(3)
    values = []
    for c in range(3):
        a = stiffness * pos[c] - damping * vel[c]
        value = vel[c] + (a * weight_sum - gathered(c)) / mass
        updated[c] = value
        values.append(value)
    keep_updated = pltpu.make_async_copy(updated, updated_h, store_sem.at[1])
    keep_updated.start()
    second = send_all(out_late, late, late_send, late_recv, local_sem.at[1], 1)
    lay_out(values, LATE_ROWS, out_late, second)

    for copy in halos[4:]:
        copy.wait()
    first_row = iota((32, DEPTH), 0) == 0
    last_row = iota((32, DEPTH), 0) == 31
    first_z = iota((32, DEPTH), 1) == 0
    last_z = iota((32, DEPTH), 1) == DEPTH - 1
    for ix in range(4):
        for c in range(3):
            f = fluid[c, ix]
            below = xlo[c] if ix == 0 else fluid[c, ix - 1]
            above = xhi[c] if ix == 3 else fluid[c, ix + 1]
            at = c * 4 + ix
            near = jnp.where(first_row, ylo[at : at + 1, :], pltpu.roll(f, 1, 0))
            far = jnp.where(last_row, yhi[at : at + 1, :], pltpu.roll(f, 31, 0))
            down = jnp.where(first_z, 0.0, pltpu.roll(f, 1, 1))
            up = jnp.where(last_z, 0.0, pltpu.roll(f, DEPTH - 1, 1))
            around = above + below
            around = around + far + near
            around = around + up + down
            spread[c, ix] = f + viscosity * (around - 6.0 * f)
    keep_spread = pltpu.make_async_copy(spread, spread_h, store_sem.at[2])
    keep_spread.start()
    for copy in sum(first + second, []) + [keep_slots, keep_updated, keep_spread]:
        copy.wait()


def particles(home, partner, pos, vel, rad, cell, route, glist, fluid):
    sds = jax.ShapeDtypeStruct
    return pl.pallas_call(
        particle_kernel,
        out_shape=(
            sds((3, NB, BLK), F32),
            sds((8, BLK), jnp.int32),
            sds((CODES, EARLY_ROWS, BLK), F32),
            sds((CODES, LATE_ROWS, BLK), F32),
            sds((3, 4, 32, DEPTH), F32),
        ),
        in_specs=[HBM] * 10,
        out_specs=(HBM,) * 5,
        scratch_shapes=[
            pltpu.VMEM((3, 4, 32, DEPTH), F32),
            pltpu.VMEM((3, 32, DEPTH), F32),
            pltpu.VMEM((3, 32, DEPTH), F32),
            pltpu.VMEM((16, DEPTH), F32),
            pltpu.VMEM((16, DEPTH), F32),
            pltpu.VMEM((3, NB, BLK), F32),
            pltpu.VMEM((8, BLK), jnp.int32),
            pltpu.SMEM((16,), jnp.int32),
            pltpu.SMEM((TILES,), jnp.int32),
            pltpu.SMEM((TILES,), jnp.int32),
            pltpu.VMEM((1, TILES), jnp.int32),
            pltpu.VMEM((3, NB, BLK), F32),
            pltpu.VMEM((3, NB, BLK), F32),
            pltpu.VMEM((NB, BLK), F32),
            pltpu.VMEM((NB, BLK), jnp.int32),
            pltpu.VMEM((1, NB), jnp.int32),
            pltpu.VMEM((3, 4, 32, DEPTH), F32),
            pltpu.VMEM((2, 2, 4, 8, BLK), F32),
            pltpu.VMEM((4, 2, 4, 8, BLK), F32),
            pltpu.VMEM((2, 16, DEPTH), F32),
            pltpu.VMEM((CAND, 8, BLK), F32),
            pltpu.VMEM((CAND, 48, BLK), BF16),
            pltpu.VMEM((CAND, 48, BLK), BF16),
            pltpu.VMEM((CAND, 32, 2 * BLK), BF16),
            pltpu.VMEM((TILES, 8, BLK), F32),
            pltpu.VMEM((4 * NB, 3 * BLK), BF16),
            pltpu.VMEM((CODES, EARLY_ROWS, BLK), F32),
            pltpu.VMEM((CODES, LATE_ROWS, BLK), F32),
            pltpu.SemaphoreType.DMA((10,)),
            pltpu.SemaphoreType.DMA((8,)),
            pltpu.SemaphoreType.DMA((8,)),
            pltpu.SemaphoreType.DMA((CODES,)),
            pltpu.SemaphoreType.DMA((CODES,)),
            pltpu.SemaphoreType.DMA((CODES,)),
            pltpu.SemaphoreType.DMA((CODES,)),
            pltpu.SemaphoreType.DMA((2,)),
            pltpu.SemaphoreType.DMA((3,)),
        ],
        compiler_params=params(56, 0),
    )(glist, home, partner, home.reshape(1, TILES), pos, vel, rad, cell, route, fluid)


def send_all(src, dst, send_sem, recv_sem, local_sem, sign):
    s, b = lax.axis_index("slab"), lax.axis_index("brick")
    copies = [[], [], []]
    for turn in ORDER:
        brick = lax.rem(b + turn, N_BRICK)
        for o in range(3):
            slab = lax.rem(s + N_SLAB + sign * (o - 1), N_SLAB)
            n = turn * 3 + o
            source = src.at[o * N_BRICK + brick]
            target = dst.at[o * N_BRICK + b]
            if turn == 0 and o == 1:
                copies[o].append(pltpu.make_async_copy(source, target, local_sem))
            else:
                copies[o].append(
                    pltpu.make_async_remote_copy(
                        src_ref=source,
                        dst_ref=target,
                        send_sem=send_sem.at[n],
                        recv_sem=recv_sem.at[n],
                        device_id=(slab, brick),
                        device_id_type=MESH,
                    )
                )
    return copies


def greet_all(barrier):
    s, b = lax.axis_index("slab"), lax.axis_index("brick")
    for turn in range(N_BRICK):
        for o in range(3):
            if turn == 0 and o == 1:
                continue
            peer = (lax.rem(s + N_SLAB + o - 1, N_SLAB), lax.rem(b + turn, N_BRICK))
            pl.semaphore_signal(barrier, inc=1, device_id=peer, device_id_type=MESH)


def return_kernel(
    slots_h, updated_h, src, out, slots, updated, back, load_sem, send_sem, recv_sem, local_sem
):
    loads = [
        pltpu.make_async_copy(slots_h.at[0], slots, load_sem.at[0]),
        pltpu.make_async_copy(updated_h, updated, load_sem.at[1]),
    ]
    for load in loads:
        load.start()
    barrier = pltpu.get_barrier_semaphore()
    greet_all(barrier)
    pl.semaphore_wait(barrier, 3 * N_BRICK - 1)
    by_offset = send_all(src, back, send_sem, recv_sem, local_sem, -1)
    copies = [copy for turn in zip(*by_offset) for copy in turn]
    for copy in copies:
        copy.start()
    for copy in loads + copies:
        copy.wait()
    for n in range(NB):
        slot = slots[n]
        code, first = slot // CAP, (slot % CAP) * 3
        for c in range(3):
            here = updated[c, n : n + 1, :]
            picked = back[code, pl.ds(first + c, 1), :]
            out[c, n : n + 1, :] = here + relaxation * (picked - here)


def return_answers(slots, updated, answers):
    return pl.pallas_call(
        return_kernel,
        out_shape=jax.ShapeDtypeStruct((3, NB, BLK), F32),
        in_specs=[HBM] * 3,
        out_specs=VMEM,
        scratch_shapes=[
            pltpu.SMEM((BLK,), jnp.int32),
            pltpu.VMEM((3, NB, BLK), F32),
            pltpu.VMEM((CODES, BACK_ROWS, BLK), F32),
            pltpu.SemaphoreType.DMA((2,)),
            pltpu.SemaphoreType.DMA((CODES,)),
            pltpu.SemaphoreType.DMA((CODES,)),
            pltpu.SemaphoreType.DMA,
        ],
        compiler_params=params(53.5, 1),
    )(slots, updated, answers)


def fluid_kernel(
    early_h,
    late_h,
    fluid_h,
    spread_h,
    next_h,
    answers_h,
    early,
    late,
    fluid,
    spread,
    answers,
    fluid_next,
    order,
    acc,
    halves,
    load_sem,
    store_sem,
):
    pairs = (
        (early_h, early.at[pl.ds(0, CODES)]),
        (late_h, late.at[pl.ds(0, CODES)]),
        (fluid_h, fluid),
        (spread_h, spread),
    )
    loads = [pltpu.make_async_copy(a, z, load_sem.at[n]) for n, (a, z) in enumerate(pairs)]
    for load in loads:
        load.start()
    acc[...] = jnp.zeros_like(acc)
    for load in loads[:2]:
        load.wait()
    valid = jnp.zeros((CODES, 1), F32)
    for k in range(CAP):
        cells = early[0:CODES, 2 * k + 1, :]
        valid = valid + jnp.where(cells[:, 0:1] > 0.5, 1.0, 0.0)
    counted = valid.astype(jnp.int32)
    offset = []
    total = jnp.int32(0)
    for d in range(CODES):
        offset.append(total)
        total = total + counted[d, 0]
    for d in range(CODES):
        for k in range(CAP):
            order[offset[d] + k] = d * 8 + k
    for n in range(SMALL):
        order[total + n] = CODES * 8
    early[CODES] = jnp.zeros((EARLY_ROWS, BLK), F32)
    late[CODES] = jnp.zeros((LATE_ROWS, BLK), F32)
    counts = [total // CHUNKS[0]]
    left_over = total - counts[0] * CHUNKS[0]
    for size in CHUNKS[1:]:
        counts.append((left_over + SMALL - 1) // size)
        left_over = jnp.maximum(left_over - counts[-1] * size, 0)

    def in_chunks(run):
        first = 0
        for count, size in zip(counts, CHUNKS):

            def step(n, _):
                run(first + n * size, size)
                return 0

            lax.fori_loop(0, count, step, 0)
            first = first + count * size

    def place(n):
        at = order[n]
        return at >> 3, at & 7

    def cells_of(d, k):
        cell = early[d, pl.ds(2 * k + 1, 1), :].astype(jnp.int32) - 1
        return cell >> 9, cell & (DEPTH - 1)

    col_iota = iota((COLS, BLK), 0)
    z_sub = iota((DEPTH, BLK), 0)
    z_lane = iota((BLK, DEPTH), 1)

    def deposit(first, count):
        left, right = [[], []], []
        for n in range(count):
            d, k = place(first + n)
            col, level = cells_of(d, k)
            radius = early[d, pl.ds(2 * k, 1), :]
            mass = radius * radius * radius
            hot = jnp.where(col_iota == col, 1.0, 0.0).astype(BF16)
            pieces = [split2(x) for x in [mass] + [mass * late[d, pl.ds(3 * k + c, 1), :] for c in range(3)]]
            for which in range(2):
                left[which].append(jnp.concatenate([hot * p[which] for p in pieces], axis=0))
            depth_tile = jnp.broadcast_to(level.astype(F32), (BLK, BLK))
            column = jnp.transpose(depth_tile).astype(jnp.int32)
            wide = jnp.concatenate([column] * (DEPTH // BLK), axis=1)
            right.append(jnp.where(wide == z_lane, 1.0, 0.0).astype(BF16))
        tall = jnp.concatenate([jnp.concatenate(x, axis=1) for x in left], axis=0)
        both = jnp.dot(tall, jnp.concatenate(right, axis=0), preferred_element_type=F32)
        acc[...] += both[0 : 4 * COLS] + both[4 * COLS : 8 * COLS]

    in_chunks(deposit)
    for load in loads[2:]:
        load.wait()

    for ix in range(4):
        base = ix * 32
        volume = acc[base : base + 32, :]
        for c in range(3):
            f = fluid[c, ix]
            start = (c + 1) * COLS + base
            momentum = acc[start : start + 32, :]
            value = spread[c, ix] + coupling * (momentum - volume * f)
            fluid_next[c, ix] = value
            high, low = split2(value)
            halves[c * COLS + base : c * COLS + base + 32, :] = high
            halves[(3 + c) * COLS + base : (3 + c) * COLS + base + 32, :] = low
    store = pltpu.make_async_copy(fluid_next, next_h, store_sem)
    store.start()

    def sample(first, count):
        hots, cols = [], []
        for n in range(count):
            col, level = cells_of(*place(first + n))
            hots.append(jnp.where(z_sub == level, 1.0, 0.0).astype(BF16))
            cols.append(col_iota == col)
        along = jnp.dot(
            halves[...], jnp.concatenate(hots, axis=1), preferred_element_type=F32
        )
        for n in range(count):
            d, k = place(first + n)
            for c in range(3):
                part = along[:, n * BLK : (n + 1) * BLK]
                both = part[c * COLS : (c + 1) * COLS] + part[(3 + c) * COLS : (4 + c) * COLS]
                value = jnp.sum(jnp.where(cols[n], both, 0.0), axis=0, keepdims=True)
                answers[d, pl.ds(3 * k + c, 1), :] = value

    in_chunks(sample)
    back = pltpu.make_async_copy(answers.at[pl.ds(0, CODES)], answers_h, load_sem.at[0])
    back.start()
    store.wait()
    back.wait()


def advance(early, late, fluid, spread):
    sds = jax.ShapeDtypeStruct
    room = CODES * CAP + CAP + SMALL
    return pl.pallas_call(
        fluid_kernel,
        out_shape=(sds((3, 4, 32, DEPTH), F32), sds((CODES, BACK_ROWS, BLK), F32)),
        in_specs=[HBM] * 4,
        out_specs=(HBM, HBM),
        scratch_shapes=[
            pltpu.VMEM((CODES + 1, EARLY_ROWS, BLK), F32),
            pltpu.VMEM((CODES + 1, LATE_ROWS, BLK), F32),
            pltpu.VMEM((3, 4, 32, DEPTH), F32),
            pltpu.VMEM((3, 4, 32, DEPTH), F32),
            pltpu.VMEM((CODES + 1, BACK_ROWS, BLK), F32),
            pltpu.VMEM((3, 4, 32, DEPTH), F32),
            pltpu.SMEM((room,), jnp.int32),
            pltpu.VMEM((4 * COLS, DEPTH), F32),
            pltpu.VMEM((6 * COLS, DEPTH), BF16),
            pltpu.SemaphoreType.DMA((4,)),
            pltpu.SemaphoreType.DMA,
        ],
        compiler_params=params(56),
    )(early, late, fluid, spread)


def on_device(
    positions, velocities, radii, cell_of, block_route, ghost_list, tile_home, tile_partner, fluid
):
    pos = jnp.transpose(positions, (1, 0, 2))
    vel = jnp.transpose(velocities, (1, 0, 2))
    route = jnp.transpose(block_route, (1, 0))
    updated, slots, early, late, spread = particles(
        tile_home, tile_partner, pos, vel, radii, cell_of, route, ghost_list, fluid
    )
    fluid_next, answers = advance(early, late, fluid, spread)
    velocity_next = return_answers(slots, updated, answers)
    return jnp.transpose(velocity_next, (1, 0, 2)), fluid_next


def solution(mesh):
    placed = (
        P(("slab", "brick"), None, None),
        P(("slab", "brick"), None, None),
        P(("slab", "brick"), None),
        P(("slab", "brick"), None),
        P(("slab", "brick"), None),
        P(("slab", "brick")),
        P(("slab", "brick")),
        P(("slab", "brick")),
        P(None, "slab", "brick", None),
    )
    return jax.shard_map(
        on_device,
        mesh=mesh,
        in_specs=placed,
        out_specs=(P(("slab", "brick"), None, None), P(None, "slab", "brick", None)),
        check_vma=False,
    )
```
